128 devices in a mesh: row: 8 (over y, core), col: 16 (over x, z).
Axes of the slice: x: 4, y: 4, z: 4, core: 2. Of those that a mesh axis runs over, the one named last changes fastest.
Arguments:
- features: bfloat16 [262144, 128], P(('row', 'col')), may hold values from -6 to 6
- new_index: int32 [262144], P(('row', 'col')), may hold values from 0 to 262143, as said below
- tile_values: bfloat16 [8, 16, 640, 128, 128], P('row', 'col'), may hold values from -0.125 to 0.125
- tile_index: int32 [8, 16, 2, 640], P('row', 'col'), may hold values from 0 to 255, as said below
- tile_count: int32 [8, 16], P('row', 'col'), may hold values from 80 to 640, as said below
- weight: bfloat16 [128, 256], replicated, may hold values from -0.5 to 0.5
- bias: float32 [256], replicated, may hold values from -3 to 3
Outputs:
- hidden: bfloat16 [262144, 256], P(('row', 'col'))
The draws below stay inside these ranges and needn't reach their ends.
Inputs may be any that keep to these rules, and one draw needn't show every extreme that they name: A permutation. The new owner of a vertex is k = new_index // 2048; owner k is the device at grid row k mod the number of grid rows and grid column k div that number. From one device to one new owner at most 32 vertices move, and exactly 32 do for some pair in every draw. `tile_index`: entry 0 of a slot is a row tile below 256, entry 1 a column tile below 128; the slots of one grid block name distinct tiles. `tile_count`: some grid block holds 640 nonzero tiles in every draw.
All inputs are finite; a program needn't handle non-finite values.
Results may differ from the reference program's by a relative error of at most 0.017.
Values may be sent and summed in bfloat16 or wider, within the bound.
No kernel may reach another device: no remote copies, remote signals or barrier semaphores. Data moves between devices by JAX's collectives and lax.ppermute only.
A program may use at most 128 MiB of HBM per device.

```python
import jax
import jax.numpy as jnp
from jax import lax

FIN = 128
HID = 256
TILE = 128
VDEV = 2048
MT = 640
N = 262144
ROWT = 256
COLT = 128
N_ROW = 8
N_COL = 16


def draw_new_index(key, part):
    owners = N // VDEV
    share = VDEV // owners
    key_spread, key_shift, key_source, key_target = jax.random.split(jax.random.fold_in(key, 11), 4)
    spread = jax.random.randint(key_spread, (owners // 2,), 0, share + 1).astype(jnp.int32).at[0].set(share)
    group_sizes = jnp.stack([share + spread, share - spread], axis=1).reshape(owners).astype(jnp.int32)
    shifts = jax.random.permutation(key_shift, owners).astype(jnp.int32)
    inverse_shift = jnp.zeros((owners,), jnp.int32).at[shifts].set(jnp.arange(owners, dtype=jnp.int32))
    group_ends = jnp.cumsum(group_sizes).astype(jnp.int32)
    group_starts = group_ends - group_sizes
    positions = jnp.arange(VDEV, dtype=jnp.int32)
    group_of = jnp.sum((positions[:, None] >= group_ends[None, :]).astype(jnp.int32), axis=1)
    within = positions - group_starts[group_of]
    sources = jnp.arange(owners, dtype=jnp.int32)
    incoming = group_sizes[inverse_shift[(sources[:, None] - sources[None, :]) % owners]]
    offsets = (jnp.cumsum(incoming, axis=1) - incoming).astype(jnp.int32)
    receivers = (sources[:, None] + shifts[group_of][None, :]) % owners
    places = offsets[receivers, sources[:, None]] + within[None, :]
    target_orders = jax.vmap(lambda one_key: jax.random.permutation(one_key, VDEV))(jax.random.split(key_target, owners)).astype(jnp.int32)
    source_orders = jax.vmap(lambda one_key: jax.random.permutation(one_key, VDEV))(jax.random.split(key_source, owners)).astype(jnp.int32)
    values = receivers * VDEV + target_orders[receivers, places]
    result = jnp.zeros((owners, VDEV), jnp.int32).at[sources[:, None], source_orders].set(values)
    return result.reshape(N)


def draw_tile_index(key, part):
    blocks = N_ROW * N_COL
    keys = jax.random.split(jax.random.fold_in(key, 23), blocks)
    chosen = jax.vmap(lambda one_key: jax.random.permutation(one_key, ROWT * COLT)[:MT])(keys).astype(jnp.int32)
    result = jnp.stack([chosen // COLT, chosen % COLT], axis=1)
    return result.reshape(N_ROW, N_COL, 2, MT).astype(jnp.int32)


def draw_tile_count(key, part):
    blocks = N_ROW * N_COL
    key_level, key_full = jax.random.split(jax.random.fold_in(key, 31))
    levels = jax.random.randint(key_level, (blocks,), 0, 4).astype(jnp.int32)
    counts = MT // jnp.left_shift(jnp.ones_like(levels), levels)
    full_block = jax.random.randint(key_full, (), 0, blocks)
    counts = counts.at[full_block].set(MT)
    return counts.reshape(N_ROW, N_COL).astype(jnp.int32)


def steps_of(rng, extent, cuts, smallest, largest):
    loudness = 1.0
    for axis_at, parts in cuts:
        heights = jax.random.uniform(jax.random.fold_in(jax.random.fold_in(rng, 6), axis_at), (parts,), jnp.float32, smallest / len(cuts), largest / len(cuts))
        loudness = loudness * jnp.repeat(jnp.exp(heights), extent[axis_at] // parts).reshape((-1,) + (1,) * (len(extent) - 1 - axis_at))
    return loudness


def centred(own_key, dims, width, most, shards=(), kind=jnp.bfloat16):
    entries = jax.random.normal(own_key, dims, jnp.float32) * width
    if len(shards) > 0:
        entries = steps_of(own_key, dims, shards, -0.22, 0.18) * entries
    return jnp.clip(entries, min=-most, max=most).astype(kind)


def setup_inputs(seed: int = 0) -> dict:
    key_of = jax.random.split(jax.random.key(seed), 8)
    features = centred(key_of[0], (N, FIN), 1.0, 6.0, ((0, 128),))
    new_index = draw_new_index(jax.random.fold_in(key_of[7], 71), 0)
    tile_values = centred(key_of[2], (N_ROW, N_COL, MT, TILE, TILE), (MT * TILE * TILE // (2 * VDEV)) ** -0.5, 0.125, ((0, 8), (1, 16)))
    tile_index = draw_tile_index(jax.random.fold_in(key_of[7], 71), 0)
    tile_count = draw_tile_count(jax.random.fold_in(key_of[7], 71), 0)
    weight = centred(key_of[5], (FIN, HID), FIN ** -0.5, 0.5)
    bias = centred(key_of[6], (HID,), 0.5, 3.0, (), jnp.float32)
    return dict(features=features, new_index=new_index, tile_values=tile_values, tile_index=tile_index, tile_count=tile_count, weight=weight, bias=bias)


def reference(features, new_index, tile_values, tile_index, tile_count, weight, bias):
    moved_rows = jnp.zeros_like(features).at[new_index].set(features)

    def block_row(row_index):
        def add_block(totals, col_index):
            tile_set = tile_values[row_index, col_index]
            tile_coords = tile_index[row_index, col_index]
            tile_total = tile_count[row_index, col_index]
            column_block = lax.dynamic_slice_in_dim(moved_rows, col_index * (COLT * TILE), COLT * TILE, 0).reshape(COLT, TILE, FIN)
            inputs = column_block[tile_coords[1]]
            products = jnp.einsum("tab,tbf->taf", tile_set.astype(jnp.float32), inputs.astype(jnp.float32))
            live_mask = jnp.arange(MT, dtype=jnp.int32) < tile_total
            products = jnp.where(live_mask[:, None, None], products, jnp.zeros_like(products))
            block_partial = jnp.zeros((ROWT, TILE, FIN), jnp.float32).at[tile_coords[0]].add(products)
            block_partial = lax.optimization_barrier(block_partial.astype(jnp.bfloat16))
            return totals + block_partial.astype(jnp.float32), None

        totals, unused = lax.scan(add_block, jnp.zeros((ROWT, TILE, FIN), jnp.float32), jnp.arange(N_COL, dtype=jnp.int32))
        return totals

    aggregate = lax.map(block_row, jnp.arange(N_ROW, dtype=jnp.int32)).reshape(N, FIN)
    rounded = aggregate.astype(jnp.bfloat16)
    hidden = jnp.dot(rounded, weight, preferred_element_type=jnp.float32) + bias
    return jnp.maximum(hidden, 0.0).astype(jnp.bfloat16)
```

```python
import functools

import jax
import jax.numpy as jnp
from jax import lax
from jax.experimental import pallas as pl
from jax.experimental.pallas import tpu as pltpu
from jax.sharding import PartitionSpec as P

BLOCK = 64
UNROLL = 16


def tile_kernel(row_tiles, count_ref, index_ref, x_ref, tiles_ref, out_ref, totals):
    edge = tiles_ref.shape[1]
    first = pl.program_id(0) * BLOCK
    count = count_ref[0]

    @pl.when(pl.program_id(0) == 0)
    def _():
        totals[...] = jnp.zeros_like(totals)

    def add_group(group, carry):
        for step in range(UNROLL):
            slot = group * UNROLL + step
            row = jnp.where(first + slot < count, index_ref[0, first + slot], row_tiles)
            col = index_ref[1, first + slot]
            product = jnp.dot(
                tiles_ref[slot],
                x_ref[pl.ds(pl.multiple_of(col * edge, edge), edge), :],
                preferred_element_type=jnp.float32,
            )
            totals[pl.ds(pl.multiple_of(row * edge, edge), edge), :] += product
        return carry

    groups = jnp.clip((count - first + UNROLL - 1) // UNROLL, 0, BLOCK // UNROLL)
    lax.fori_loop(0, groups, add_group, 0)

    @pl.when(pl.program_id(0) == pl.num_programs(0) - 1)
    def _():
        out_ref[...] = totals[: row_tiles * edge, :].astype(out_ref.dtype)


def tile_products(count, index, x, tiles, rows):
    slots, edge, _ = tiles.shape
    width = x.shape[1]
    row_tiles = rows // edge

    def tile_block(step, count_ref, index_ref):
        return jnp.minimum(step, jnp.maximum(count_ref[0] - 1, 0) // BLOCK), 0, 0

    return pl.pallas_call(
        functools.partial(tile_kernel, row_tiles),
        out_shape=jax.ShapeDtypeStruct((rows, width), jnp.bfloat16),
        grid_spec=pltpu.PrefetchScalarGridSpec(
            num_scalar_prefetch=2,
            grid=(slots // BLOCK,),
            in_specs=[
                pl.BlockSpec(x.shape, lambda *_: (0, 0), pipeline_mode=pl.Buffered(1)),
                pl.BlockSpec((BLOCK, edge, edge), tile_block),
            ],
            out_specs=pl.BlockSpec(
                (rows, width), lambda *_: (0, 0), pipeline_mode=pl.Buffered(1)
            ),
            scratch_shapes=[pltpu.VMEM((rows + edge, width), jnp.float32)],
        ),
        compiler_params=pltpu.CompilerParams(vmem_limit_bytes=56 << 20),
        name="tile_products",
    )(count, index, x, tiles)


def body(features, new_index, tile_values, tile_index, tile_count, weight, bias):
    grid_rows = lax.axis_size("row")
    grid_cols = lax.axis_size("col")
    device_total = grid_rows * grid_cols
    local_rows = features.shape[0]
    feature_width = features.shape[1]
    capacity = 2 * local_rows // device_total
    new_owner = new_index // local_rows
    new_slot = new_index % local_rows
    target_peer = new_owner % grid_rows * grid_cols + new_owner // grid_rows
    peer_hits = (target_peer[:, None] == jnp.arange(device_total, dtype=jnp.int32)[None, :]).astype(
        jnp.int32
    )
    peer_rank = jnp.sum((jnp.cumsum(peer_hits, axis=0) - peer_hits) * peer_hits, axis=1)
    outgoing = (
        jnp.zeros((device_total, capacity, feature_width), jnp.bfloat16)
        .at[target_peer, peer_rank]
        .set(features)
    )
    slots_out = (
        jnp.full((device_total, capacity), local_rows, jnp.int32)
        .at[target_peer, peer_rank]
        .set(new_slot)
    )
    rows_in, slots_in = (
        lax.all_to_all(outgoing, ("row", "col"), split_axis=0, concat_axis=0, tiled=True),
        lax.all_to_all(slots_out, ("row", "col"), split_axis=0, concat_axis=0, tiled=True),
    )
    moved_rows = (
        jnp.zeros((local_rows, feature_width), jnp.bfloat16)
        .at[slots_in.reshape(-1)]
        .set(rows_in.reshape(-1, feature_width), mode="drop")
    )
    column_block = lax.all_gather(moved_rows, "row", axis=0, tiled=True)
    tile_set = tile_values[0, 0]
    partial_rows = tile_products(
        tile_count.reshape(1), tile_index[0, 0], column_block, tile_set, local_rows * grid_cols
    )
    row_totals = lax.psum_scatter(
        partial_rows, "col", scatter_dimension=0, tiled=True
    )
    hidden = jnp.dot(row_totals, weight, preferred_element_type=jnp.float32) + bias
    return jnp.maximum(hidden, 0.0).astype(jnp.bfloat16)


def solution(mesh):
    in_specs = (
        P(("row", "col"), None),
        P(("row", "col")),
        P("row", "col", None, None, None),
        P("row", "col", None, None),
        P("row", "col"),
        P(),
        P(),
    )
    out_specs = P(("row", "col"), None)
    return jax.shard_map(body, mesh=mesh, in_specs=in_specs, out_specs=out_specs, check_vma=False)
```

```python
import functools

import jax
import jax.numpy as jnp
from jax import lax
from jax.experimental import pallas as pl
from jax.experimental.pallas import tpu as pltpu
from jax.sharding import Mesh
from jax.sharding import PartitionSpec as P

EXTRA = 8
PICK = 256
UNROLL = 16
SLOTS = 6
STREAMS = 4
SIDE = 4
LANES = 128
F32 = jnp.float32
BF16 = jnp.bfloat16


def iota(shape, axis):
    return lax.broadcasted_iota(jnp.int32, shape, axis)


def log2(size):
    assert size & (size - 1) == 0
    return size.bit_length() - 1


def params(mib, **rest):
    return pltpu.CompilerParams(vmem_limit_bytes=mib << 20, **rest)


VMEM = pl.BlockSpec(memory_space=pltpu.VMEM)
SMEM = pl.BlockSpec(memory_space=pltpu.SMEM)


def pack_kernel(grid_rows, grid_cols, capacity, index_ref, rows_ref, out_ref):
    local_rows, width = rows_ref.shape
    peers = grid_rows * grid_cols
    lower = (iota((LANES, LANES), 0) < iota((LANES, LANES), 1)).astype(F32).astype(BF16)
    nt = (((1,), (1,)), ((), ()))
    seen = jnp.zeros((peers, 1), F32)
    high = jnp.zeros((peers, LANES), F32)
    low = jnp.zeros((peers, LANES), F32)
    zero = jnp.zeros((LANES, LANES), F32)
    places = []
    for block in range(local_rows // LANES):
        index = index_ref[block : block + 1, :]
        owner = index >> log2(local_rows)
        slot = index & (local_rows - 1)
        peer = (owner & (grid_rows - 1)) * grid_cols + (owner >> log2(grid_rows))
        hit = (iota((peers, LANES), 0) == peer).astype(F32)
        hit16 = hit.astype(BF16)
        before = jnp.dot(hit16, lower, preferred_element_type=F32) + seen
        rank = jnp.sum(before * hit, axis=0, keepdims=True).astype(jnp.int32)
        seen = seen + jnp.sum(hit, axis=1, keepdims=True)
        places.append(peer * capacity + rank)
        same = (iota((LANES, LANES), 0) & (capacity - 1)) == rank
        slot_high = jnp.where(same, ((slot >> 7) + 1).astype(F32), zero).astype(BF16)
        slot_low = jnp.where(same, (slot & 127).astype(F32), zero).astype(BF16)
        high += lax.dot_general(hit16, slot_high, nt, preferred_element_type=F32)
        low += lax.dot_general(hit16, slot_low, nt, preferred_element_type=F32)
    place = jnp.concatenate(places, axis=1)
    part = PICK // capacity

    def pick_rows(step, carry):
        pick = (iota((PICK, local_rows), 0) + step * PICK == place).astype(F32).astype(BF16)
        rows = jnp.dot(pick, rows_ref[...], preferred_element_type=F32).astype(BF16)
        out_ref[pl.ds(step * part, part), 0:capacity, :] = rows.reshape(part, capacity, width)
        return carry

    lax.fori_loop(0, peers * capacity // PICK, pick_rows, 0)
    at = iota((peers, EXTRA, LANES), 1)
    none = jnp.zeros((peers, EXTRA, LANES), F32)
    extra = jnp.where(
        at == 0,
        high.reshape(peers, 1, LANES) + none,
        jnp.where(at == 1, low.reshape(peers, 1, LANES) + none, none),
    )
    out_ref[:, capacity:, :] = extra.astype(BF16)


def pack_rows(index, rows, grid_rows, grid_cols, capacity):
    peers = grid_rows * grid_cols
    return pl.pallas_call(
        functools.partial(pack_kernel, grid_rows, grid_cols, capacity),
        out_shape=jax.ShapeDtypeStruct((peers, capacity + EXTRA, rows.shape[1]), BF16),
        in_specs=[VMEM] * 2,
        out_specs=VMEM,
        compiler_params=params(32),
        name="pack_rows",
    )(index.reshape(-1, LANES), rows)


def place_kernel(in_ref, out_ref, slot_ref, rows_ref):
    peers, held, width = in_ref.shape
    capacity = held - EXTRA
    local_rows = out_ref.shape[0]
    per = LANES // capacity
    extra = in_ref[:, capacity:, :].astype(F32)
    high, low = extra[:, 0, :], extra[:, 1, :]
    slot_ref[...] = jnp.where(high > 0.5, (high - 1.0) * 128.0 + low, -1.0)
    rows_ref[...] = in_ref[:, 0:capacity, :].reshape(peers * capacity, width)
    which = iota((peers // per, LANES), 1) >> log2(capacity)
    slot = jnp.zeros((peers // per, LANES), F32)
    for i in range(per):
        slot = jnp.where(which == i, slot_ref[pl.ds(i, peers // per, stride=per), :], slot)
    slot = slot.astype(jnp.int32)
    slot = jnp.concatenate([slot[q : q + 1, :] for q in range(peers // per)], axis=1)

    def place_rows(step, carry):
        pick = (iota((PICK, peers * capacity), 0) + step * PICK == slot).astype(F32).astype(BF16)
        rows = jnp.dot(pick, rows_ref[...], preferred_element_type=F32)
        out_ref[pl.ds(pl.multiple_of(step * PICK, PICK), PICK), :] = rows.astype(BF16)
        return carry

    lax.fori_loop(0, local_rows // PICK, place_rows, 0)


def place_rows(got, local_rows):
    peers, held, width = got.shape
    return pl.pallas_call(
        place_kernel,
        out_shape=jax.ShapeDtypeStruct((local_rows, width), BF16),
        in_specs=[VMEM],
        out_specs=VMEM,
        scratch_shapes=[
            pltpu.VMEM((peers, LANES), F32),
            pltpu.VMEM((peers * (held - EXTRA), width), BF16),
        ],
        compiler_params=params(32),
        name="place_rows",
    )(got)


def plan_kernel(row_tiles, me_ref, count_ref, index_ref, slot_ref, row_ref, col_ref, size_ref):
    me_x, me_z = me_ref[0], me_ref[1]
    half = row_tiles // 2
    groups = (0b01111000, 0b10110100)

    def group_of(delta, pairing):
        table = jnp.where(pairing == 0, groups[0], groups[1])
        return (table >> (2 * delta)) & 3

    def visit(tile, sizes):
        row, col = index_ref[0, tile], index_ref[1, tile]
        dest, inner = row // 16, row % 16
        stream, sub = inner // 4, inner % 4
        d_x, d_z = (dest // SIDE) ^ me_x, (dest % SIDE) ^ me_z
        first = jnp.where(stream < 2, d_x, d_z)
        second = jnp.where(stream < 2, d_z, d_x)
        g_1 = group_of(first, stream % 2)
        g_2 = group_of(second, stream % 2)
        kept = jnp.where(g_1 < 2, 1, 0)
        place = stream * 32 + (g_1 % 2) * 16 + g_2 * 4 + sub
        at = jnp.where(kept == 1, sizes[1], sizes[0])
        slot_ref[kept, at] = tile
        row_ref[kept, at] = place
        col_ref[kept, at] = col
        return sizes[0] + 1 - kept, sizes[1] + kept

    sizes = lax.fori_loop(0, count_ref[0], visit, (jnp.int32(0), jnp.int32(0)))
    for kept in range(2):
        size_ref[kept] = (sizes[kept] + UNROLL - 1) // UNROLL
        for step in range(UNROLL):
            slot_ref[kept, sizes[kept] + step] = 0
            row_ref[kept, sizes[kept] + step] = half
            col_ref[kept, sizes[kept] + step] = 0


def plan_tiles(me, count, index, row_tiles):
    slots = index.shape[1] + UNROLL
    table = jax.ShapeDtypeStruct((2, slots), jnp.int32)
    return pl.pallas_call(
        functools.partial(plan_kernel, row_tiles),
        out_shape=[table, table, table, jax.ShapeDtypeStruct((2,), jnp.int32)],
        in_specs=[SMEM] * 3,
        out_specs=[SMEM] * 4,
        name="plan_tiles",
    )(me, count, index)


def tile_kernel(kept, slot_ref, row_ref, col_ref, size_ref, x_ref, tiles_ref, *refs):
    out_refs, (held, totals, sems) = refs[:STREAMS], refs[STREAMS:]
    edge = held.shape[2]
    groups = size_ref[kept]

    def fetch(group):
        lane = lax.rem(group, SLOTS)
        for step in range(UNROLL):
            tile = slot_ref[kept, group * UNROLL + step]
            pltpu.make_async_copy(tiles_ref.at[tile], held.at[lane, step], sems.at[lane]).start()

    for ahead in range(SLOTS - 1):

        @pl.when(ahead < groups)
        def _():
            fetch(ahead)

    totals[...] = jnp.zeros_like(totals)

    def add_group(group, carry):
        @pl.when(group + SLOTS - 1 < groups)
        def _():
            fetch(group + SLOTS - 1)

        lane = lax.rem(group, SLOTS)
        pltpu.make_async_copy(tiles_ref.at[pl.ds(0, UNROLL)], held.at[lane], sems.at[lane]).wait()
        for step in range(UNROLL):
            row = row_ref[kept, group * UNROLL + step]
            col = col_ref[kept, group * UNROLL + step]
            product = jnp.dot(
                held[lane, step],
                x_ref[pl.ds(pl.multiple_of(col * edge, edge), edge), :],
                preferred_element_type=F32,
            )
            totals[pl.ds(pl.multiple_of(row * edge, edge), edge), :] += product
        return carry

    lax.fori_loop(0, groups, add_group, 0)
    rows = out_refs[0].shape[0]
    for stream, out_ref in enumerate(out_refs):
        out_ref[...] = totals[stream * rows : (stream + 1) * rows, :].astype(BF16)


def tile_products(kept, plan, x, tiles, row_tiles):
    _, edge, _ = tiles.shape
    width = x.shape[1]
    half = row_tiles // 2 * edge
    return pl.pallas_call(
        functools.partial(tile_kernel, kept),
        out_shape=[jax.ShapeDtypeStruct((half // STREAMS, width), BF16)] * STREAMS,
        in_specs=[SMEM] * 4 + [VMEM, pl.BlockSpec(memory_space=pl.ANY)],
        out_specs=[VMEM] * STREAMS,
        scratch_shapes=[
            pltpu.VMEM((SLOTS, UNROLL, edge, edge), BF16),
            pltpu.VMEM((half + edge, width), F32),
            pltpu.SemaphoreType.DMA((SLOTS,)),
        ],
        compiler_params=params(32),
        cost_estimate=pl.CostEstimate(
            flops=40_000_000_000, bytes_accessed=40_000_000, transcendentals=0
        ),
        name="tile_products",
    )(*plan, x, tiles)


def wide(ref, start, rows):
    return ref[start : start + rows, :].astype(F32)


def forward_kernel(*refs):
    for stream in range(STREAMS):
        kept, got, out = refs[2 * stream], refs[2 * stream + 1], refs[2 * STREAMS + stream]
        rows = out.shape[0]
        out[...] = (wide(kept, rows, rows) + wide(got, rows, rows)).astype(BF16)


def forward_sums(kept, got):
    pairs = [array for pair in zip(kept, got) for array in pair]
    out = jax.ShapeDtypeStruct((kept[0].shape[0] // 2, kept[0].shape[1]), BF16)
    return pl.pallas_call(
        forward_kernel,
        out_shape=[out] * STREAMS,
        in_specs=[VMEM] * len(pairs),
        out_specs=[VMEM] * STREAMS,
        compiler_params=params(32),
        name="forward_sums",
    )(*pairs)


def turn_kernel(*refs):
    for stream in range(STREAMS):
        kept, got, last = refs[3 * stream : 3 * stream + 3]
        keep, send = refs[3 * STREAMS + 2 * stream : 3 * STREAMS + 2 * stream + 2]
        rows = last.shape[0] // 2
        for out, start in ((keep, 0), (send, rows)):
            total = wide(kept, start, rows) + wide(got, start, rows) + wide(last, start, rows)
            out[...] = total.astype(out.dtype)


def turn_sums(kept, got, last):
    ins = [array for three in zip(kept, got, last) for array in three]
    rows, width = last[0].shape
    outs = [
        jax.ShapeDtypeStruct((rows // 2, width), F32),
        jax.ShapeDtypeStruct((rows // 2, width), BF16),
    ] * STREAMS
    done = pl.pallas_call(
        turn_kernel,
        out_shape=outs,
        in_specs=[VMEM] * len(ins),
        out_specs=[VMEM] * len(outs),
        compiler_params=params(32),
        name="turn_sums",
    )(*ins)
    return done[0::2], done[1::2]


def dense_kernel(*refs):
    weight_ref, bias_ref, out_ref = refs[3 * STREAMS :]
    for stream in range(STREAMS):
        kept, got, last = refs[3 * stream : 3 * stream + 3]
        rows = last.shape[0]
        total = wide(kept, 0, rows) + wide(got, 0, rows) + wide(last, 0, rows)
        hidden = jnp.dot(total.astype(BF16), weight_ref[...], preferred_element_type=F32)
        hidden = jnp.maximum(hidden + bias_ref[...], 0.0)
        out_ref[stream * rows : (stream + 1) * rows, :] = hidden.astype(BF16)


def dense(kept, got, last, weight, bias):
    ins = [array for three in zip(kept, got, last) for array in three]
    rows = last[0].shape[0] * STREAMS
    return pl.pallas_call(
        dense_kernel,
        out_shape=jax.ShapeDtypeStruct((rows, weight.shape[1]), BF16),
        in_specs=[VMEM] * (len(ins) + 2),
        out_specs=VMEM,
        compiler_params=params(32),
        name="dense",
    )(*ins, weight, bias.reshape(1, -1))


def swap(arrays, axes, first):
    out = []
    for stream, array in enumerate(arrays):
        bits = (1, 3) if stream % 2 == 0 else (3, 1)
        bit = bits[0] if first else bits[1]
        axis = axes[0] if stream < 2 else axes[1]
        out.append(lax.ppermute(array, axis, [(c, c ^ bit) for c in range(SIDE)]))
    return out


def body(features, new_index, tile_values, tile_index, tile_count, weight, bias):
    grid_rows = lax.axis_size("y") * lax.axis_size("core")
    grid_cols = lax.axis_size("x") * lax.axis_size("z")
    local_rows = features.shape[0]
    everyone = ("y", "core", "x", "z")
    capacity = 2 * local_rows // (grid_rows * grid_cols)
    tiles = tile_values[0, 0]
    row_tiles = local_rows * grid_cols // tiles.shape[1]
    assert row_tiles == 256 and grid_cols == SIDE * SIDE

    me = jnp.stack([lax.axis_index("x"), lax.axis_index("z")]).astype(jnp.int32)
    plan = plan_tiles(me, tile_count.reshape(1), tile_index[0, 0], row_tiles)
    packed = pack_rows(new_index, features, grid_rows, grid_cols, capacity)
    got = lax.all_to_all(packed, everyone, split_axis=0, concat_axis=0, tiled=True)
    moved_rows = place_rows(got, local_rows)
    column_block = lax.all_gather(moved_rows, ("y", "core"), axis=0, tiled=True)

    sent = tile_products(0, plan, column_block, tiles, row_tiles)
    got_1 = swap(sent, ("x", "z"), True)
    kept = tile_products(1, plan, column_block, tiles, row_tiles)
    got_2 = swap(forward_sums(kept, got_1), ("x", "z"), False)
    keep, send = turn_sums(kept, got_1, got_2)
    got_3 = swap(send, ("z", "x"), True)
    got_4 = swap(forward_sums(keep, got_3), ("z", "x"), False)
    return dense(keep, got_3, got_4, weight, bias)


def solution(mesh):
    fine = Mesh(mesh.devices.reshape(-1, 2, SIDE, SIDE), ("y", "core", "x", "z"))
    grid = (("y", "core"), ("x", "z"))
    flat = ("y", "core", "x", "z")
    in_specs = (
        P(flat, None),
        P(flat),
        P(*grid, None, None, None),
        P(*grid, None, None),
        P(*grid),
        P(),
        P(),
    )
    return jax.shard_map(
        body, mesh=fine, in_specs=in_specs, out_specs=P(flat, None), check_vma=False
    )
```

```python
import functools

import jax
import jax.numpy as jnp
from jax import lax
from jax.experimental import pallas as pl
from jax.experimental.pallas import tpu as pltpu
from jax.sharding import Mesh
from jax.sharding import PartitionSpec as P

EXTRA = 8
PICK = 1024
UNROLL = 16
SLOTS = 6
STREAMS = 4
PAIR = 2
SIDE = 4
LANES = 128
F32 = jnp.float32
BF16 = jnp.bfloat16


def iota(shape, axis):
    return lax.broadcasted_iota(jnp.int32, shape, axis)


def log2(size):
    assert size & (size - 1) == 0
    return size.bit_length() - 1


def params(mib, **rest):
    return pltpu.CompilerParams(vmem_limit_bytes=mib << 20, **rest)


VMEM = pl.BlockSpec(memory_space=pltpu.VMEM)
SMEM = pl.BlockSpec(memory_space=pltpu.SMEM)
HBM = pl.BlockSpec(memory_space=pltpu.HBM)


def pack_kernel(
    grid_rows,
    grid_cols,
    capacity,
    index_hbm,
    rows_hbm,
    out_ref,
    index_ref,
    rows_ref,
    hits_ref,
    marks_ref,
    sems,
):
    local_rows, width = rows_ref.shape
    index_copy = pltpu.make_async_copy(index_hbm, index_ref, sems.at[0])
    index_copy.start()
    copy = pltpu.make_async_copy(rows_hbm, rows_ref, sems.at[1])
    copy.start()
    peers = grid_rows * grid_cols
    lanes = (LANES, 2 * LANES)
    earlier = jnp.where(iota(lanes, 0) < iota(lanes, 1), 1.0, 0.0).astype(BF16)
    rank_lane = iota((LANES, LANES), 0) & (capacity - 1)
    seen = jnp.zeros((peers, LANES), F32)
    zero = jnp.zeros((LANES, LANES), F32)
    places = []
    index_copy.wait()
    for block in range(local_rows // LANES):
        here = slice(block * LANES, (block + 1) * LANES)
        index = index_ref[block : block + 1, :]
        owner = index >> log2(local_rows)
        slot = index & (local_rows - 1)
        row = owner & (grid_rows - 1)
        peer = ((row & 1) * (grid_rows // 2) + (row >> 1)) * grid_cols + (owner >> log2(grid_rows))
        hit = jnp.where(iota((peers, LANES), 0) == peer, 1.0, 0.0)
        hits_ref[:, here] = hit.astype(BF16)
        counts = jnp.dot(hit.astype(BF16), earlier, preferred_element_type=F32)
        rank = jnp.sum((counts[:, :LANES] + seen) * hit, axis=0, keepdims=True).astype(jnp.int32)
        seen = seen + counts[:, LANES:]
        places.append(peer * capacity + rank)
        same = rank_lane == rank
        high = jnp.where(same, ((slot >> 7) + 1).astype(F32), zero)
        low = jnp.where(same, (slot & 127).astype(F32), zero)
        marks_ref[:LANES, here] = high.astype(BF16)
        marks_ref[LANES:, here] = low.astype(BF16)
    marks = lax.dot_general(
        hits_ref[...], marks_ref[...], (((1,), (1,)), ((), ())), preferred_element_type=F32
    )
    at = iota((peers, EXTRA, LANES), 1)
    none = jnp.zeros((peers, EXTRA, LANES), F32)
    extra = jnp.where(
        at == 0,
        marks[:, :LANES].reshape(peers, 1, LANES) + none,
        jnp.where(at == 1, marks[:, LANES:].reshape(peers, 1, LANES) + none, none),
    )
    out_ref[:, capacity:, :] = extra.astype(BF16)
    place = jnp.concatenate(places, axis=1)
    part = PICK // capacity
    copy.wait()

    def pick_rows(step, carry):
        pick = (iota((PICK, local_rows), 0) + step * PICK == place).astype(F32).astype(BF16)
        rows = jnp.dot(pick, rows_ref[...], preferred_element_type=F32).astype(BF16)
        out_ref[pl.ds(step * part, part), 0:capacity, :] = rows.reshape(part, capacity, width)
        return carry

    lax.fori_loop(0, peers * capacity // PICK, pick_rows, 0)


def pack_rows(index, rows, grid_rows, grid_cols, capacity):
    peers = grid_rows * grid_cols
    local_rows, width = rows.shape
    return pl.pallas_call(
        functools.partial(pack_kernel, grid_rows, grid_cols, capacity),
        out_shape=jax.ShapeDtypeStruct((peers, capacity + EXTRA, width), BF16),
        in_specs=[HBM] * 2,
        out_specs=VMEM,
        scratch_shapes=[
            pltpu.VMEM((local_rows // LANES, LANES), jnp.int32),
            pltpu.VMEM((local_rows, width), BF16),
            pltpu.VMEM((peers, local_rows), BF16),
            pltpu.VMEM((2 * LANES, local_rows), BF16),
            pltpu.SemaphoreType.DMA((2,)),
        ],
        compiler_params=params(60),
        name="pack_rows",
    )(index.reshape(-1, LANES), rows)


def place_kernel(in_ref, out_ref, slot_ref, rows_ref):
    peers, held, width = in_ref.shape
    capacity = held - EXTRA
    local_rows = out_ref.shape[0]
    per = LANES // capacity
    extra = in_ref[:, capacity:, :].astype(F32)
    high, low = extra[:, 0, :], extra[:, 1, :]
    slot_ref[...] = jnp.where(high > 0.5, (high - 1.0) * 128.0 + low, -1.0)
    rows_ref[...] = in_ref[:, 0:capacity, :].reshape(peers * capacity, width)
    which = iota((peers // per, LANES), 1) >> log2(capacity)
    slot = jnp.zeros((peers // per, LANES), F32)
    for i in range(per):
        slot = jnp.where(which == i, slot_ref[pl.ds(i, peers // per, stride=per), :], slot)
    slot = slot.astype(jnp.int32)
    slot = jnp.concatenate([slot[q : q + 1, :] for q in range(peers // per)], axis=1)

    def place_rows(step, carry):
        pick = (iota((PICK, peers * capacity), 0) + step * PICK == slot).astype(F32).astype(BF16)
        rows = jnp.dot(pick, rows_ref[...], preferred_element_type=F32)
        out_ref[pl.ds(pl.multiple_of(step * PICK, PICK), PICK), :] = rows.astype(BF16)
        return carry

    lax.fori_loop(0, local_rows // PICK, place_rows, 0)


def place_rows(got, local_rows):
    peers, held, width = got.shape
    return pl.pallas_call(
        place_kernel,
        out_shape=jax.ShapeDtypeStruct((local_rows, width), BF16),
        in_specs=[VMEM],
        out_specs=VMEM,
        scratch_shapes=[
            pltpu.VMEM((peers, LANES), F32),
            pltpu.VMEM((peers * (held - EXTRA), width), BF16),
        ],
        compiler_params=params(32),
        name="place_rows",
    )(got)


def tile_codes(index, me_x, me_z):
    row, col = index[0], index[1]
    tile = jnp.arange(index.shape[1], dtype=jnp.int32)
    dest, inner = row >> 4, row & 15
    stream, sub = inner >> 2, inner & 3
    d_x, d_z = (dest >> 2) ^ me_x, (dest & 3) ^ me_z
    first = jnp.where(stream < 2, d_x, d_z)
    second = jnp.where(stream < 2, d_z, d_x)
    near = jnp.where(stream & 1 == 0, 1, 3)
    place = stream * 16 + second * 4 + sub
    group = jnp.where(first == 0, 2, jnp.where(first == 2, 0, 1))
    place = place + jnp.where((group == 1) & (first != near), 64, 0)
    return (group << 25) | (tile << 15) | (place << 7) | col


def plan_kernel(count_ref, code_ref, table_ref):
    for group in range(3):
        table_ref[3, group] = 0

    def visit(step, carry):
        for sub in range(8):
            code = code_ref[step * 8 + sub]
            group = code >> 25
            at = table_ref[3, group]
            table_ref[group, at] = code
            table_ref[3, group] = at + 1
        return carry

    count = count_ref[0]
    full = count // 8
    lax.fori_loop(0, full, visit, 0)

    def visit_one(tile, carry):
        code = code_ref[tile]
        group = code >> 25
        at = table_ref[3, group]
        table_ref[group, at] = code
        table_ref[3, group] = at + 1
        return carry

    lax.fori_loop(full * 8, count, visit_one, 0)
    for group in range(3):
        for step in range(UNROLL):
            table_ref[group, table_ref[3, group] + step] = 128 << 7


def plan_tiles(count, codes):
    return pl.pallas_call(
        plan_kernel,
        out_shape=jax.ShapeDtypeStruct((4, codes.shape[0] + UNROLL), jnp.int32),
        in_specs=[SMEM] * 2,
        out_specs=SMEM,
        name="plan_tiles",
    )(count, codes)


def tile_kernel(group, arrays, table_ref, x_ref, tiles_ref, *refs):
    out_refs, (held, totals, sems) = refs[:arrays], refs[arrays:]
    edge = held.shape[2]
    steps = (table_ref[3, group] + UNROLL - 1) // UNROLL

    def fetch(step):
        lane = lax.rem(step, SLOTS)
        for sub in range(UNROLL):
            tile = (table_ref[group, step * UNROLL + sub] >> 15) & 1023
            pltpu.make_async_copy(tiles_ref.at[tile], held.at[lane, sub], sems.at[lane]).start()

    for ahead in range(SLOTS - 1):

        @pl.when(ahead < steps)
        def _():
            fetch(ahead)

    totals[...] = jnp.zeros_like(totals)

    def add_tiles(step, carry):
        @pl.when(step + SLOTS - 1 < steps)
        def _():
            fetch(step + SLOTS - 1)

        lane = lax.rem(step, SLOTS)
        pltpu.make_async_copy(tiles_ref.at[pl.ds(0, UNROLL)], held.at[lane], sems.at[lane]).wait()
        for sub in range(UNROLL):
            code = table_ref[group, step * UNROLL + sub]
            row = jnp.minimum((code >> 7) & 255, totals.shape[0] // edge - 1)
            col = code & 127
            product = jnp.dot(
                held[lane, sub],
                x_ref[pl.ds(pl.multiple_of(col * edge, edge), edge), :],
                preferred_element_type=F32,
            )
            totals[pl.ds(pl.multiple_of(row * edge, edge), edge), :] += product
        return carry

    lax.fori_loop(0, steps, add_tiles, 0)
    rows = out_refs[0].shape[0]
    for array, out_ref in enumerate(out_refs):
        out_ref[...] = totals[array * rows : (array + 1) * rows, :].astype(BF16)


def tile_products(group, arrays, table, x, tiles, rows):
    _, edge, _ = tiles.shape
    width = x.shape[1]
    return pl.pallas_call(
        functools.partial(tile_kernel, group, arrays),
        out_shape=[jax.ShapeDtypeStruct((rows, width), BF16)] * arrays,
        in_specs=[SMEM, VMEM, HBM],
        out_specs=[VMEM] * arrays,
        scratch_shapes=[
            pltpu.VMEM((SLOTS, UNROLL, edge, edge), BF16),
            pltpu.VMEM((arrays * rows + edge, width), F32),
            pltpu.SemaphoreType.DMA((SLOTS,)),
        ],
        compiler_params=params(32),
        cost_estimate=pl.CostEstimate(
            flops=5_000_000_000 * arrays, bytes_accessed=5_000_000 * arrays, transcendentals=0
        ),
        name="tile_products",
    )(table, x, tiles)


def wide(ref, start, rows):
    return ref[start : start + rows, :].astype(F32)


def forward_kernel(*refs):
    for stream in range(STREAMS):
        kept, got, out = refs[2 * stream], refs[2 * stream + 1], refs[2 * STREAMS + stream]
        out[...] = (kept[...].astype(F32) + got[...].astype(F32)).astype(BF16)


def forward_sums(kept, got):
    pairs = [array for pair in zip(kept, got) for array in pair]
    return pl.pallas_call(
        forward_kernel,
        out_shape=[jax.ShapeDtypeStruct(kept[0].shape, BF16)] * STREAMS,
        in_specs=[VMEM] * len(pairs),
        out_specs=[VMEM] * STREAMS,
        compiler_params=params(32),
        name="forward_sums",
    )(*pairs)


def turn_kernel(*refs):
    outs = refs[3 * STREAMS :]
    for stream in range(STREAMS):
        kept, got, last = refs[3 * stream : 3 * stream + 3]
        rows = last.shape[0] // SIDE
        at = stream % PAIR * rows
        for delta in range(SIDE):
            start = delta * rows
            total = wide(kept, start, rows) + wide(got, start, rows) + wide(last, start, rows)
            out = outs[stream // PAIR * SIDE + delta]
            out[at : at + rows, :] = total.astype(out.dtype)


def turn_sums(kept, got, last):
    ins = [array for three in zip(kept, got, last) for array in three]
    rows, width = last[0].shape
    shape = (PAIR * rows // SIDE, width)
    outs = [jax.ShapeDtypeStruct(shape, F32)] + [jax.ShapeDtypeStruct(shape, BF16)] * (SIDE - 1)
    done = pl.pallas_call(
        turn_kernel,
        out_shape=outs * 2,
        in_specs=[VMEM] * len(ins),
        out_specs=[VMEM] * (2 * SIDE),
        compiler_params=params(32),
        name="turn_sums",
    )(*ins)
    return done[:SIDE], done[SIDE:]


def dense_kernel(*refs):
    weight_ref, bias_ref, out_ref = refs[2 * SIDE :]
    for side in range(2):
        own, *got = refs[side * SIDE : (side + 1) * SIDE]
        rows = own.shape[0]
        total = own[...]
        for ref in got:
            total += ref[...].astype(F32)
        hidden = jnp.dot(total.astype(BF16), weight_ref[...], preferred_element_type=F32)
        hidden = jnp.maximum(hidden + bias_ref[...], 0.0)
        out_ref[side * rows : (side + 1) * rows, :] = hidden.astype(BF16)


def dense(terms, weight, bias):
    return pl.pallas_call(
        dense_kernel,
        out_shape=jax.ShapeDtypeStruct((2 * terms[0].shape[0], weight.shape[1]), BF16),
        in_specs=[VMEM] * (len(terms) + 2),
        out_specs=VMEM,
        compiler_params=params(32),
        name="dense",
    )(*terms, weight, bias.reshape(1, -1))


def swap(arrays, axis, first):
    return [
        lax.ppermute(array, axis, [(c, c ^ bit) for c in range(SIDE)])
        for array, bit in zip(arrays, (1, 3) if first else (3, 1))
    ]


def spread(sides):
    got = [list(side) for side in sides]
    for bit in (1, 2, 3):
        for side, axis in enumerate(("z", "x")):
            got[side][bit] = lax.ppermute(
                sides[side][bit], axis, [(c, c ^ bit) for c in range(SIDE)]
            )
    return got[0] + got[1]


def body(features, new_index, tile_values, tile_index, tile_count, weight, bias):
    grid_rows = lax.axis_size("y") * lax.axis_size("core")
    grid_cols = lax.axis_size("x") * lax.axis_size("z")
    local_rows = features.shape[0]
    everyone = ("core", "y", "x", "z")
    capacity = 2 * local_rows // (grid_rows * grid_cols)
    tiles = tile_values[0, 0]
    row_tiles = local_rows * grid_cols // tiles.shape[1]
    assert row_tiles == 256 and grid_cols == SIDE * SIDE

    codes = tile_codes(tile_index[0, 0], lax.axis_index("x"), lax.axis_index("z"))
    packed = pack_rows(new_index, features, grid_rows, grid_cols, capacity)
    got = lax.all_to_all(packed, everyone, split_axis=0, concat_axis=0, tiled=True)
    table = plan_tiles(tile_count.reshape(1), codes)
    got, table = lax.optimization_barrier((got, table))
    moved_rows = place_rows(got, local_rows)
    x = lax.all_gather(moved_rows, ("y", "core"), axis=0, tiled=True)

    rows = local_rows * grid_cols // 16
    axes = ("x", "z")
    pairs = (slice(0, PAIR), slice(PAIR, STREAMS))
    sent_on = tile_products(0, STREAMS, table, x, tiles, rows)
    got_on = [swap(sent_on[pair], axis, True) for pair, axis in zip(pairs, axes)]
    both = tile_products(1, 2 * STREAMS, table, x, tiles, rows)
    got_own = [swap(both[pair], axis, True) for pair, axis in zip(pairs, axes)]
    hand = forward_sums(both[STREAMS:], got_on[0] + got_on[1])
    got_last = [swap(hand[pair], axis, False) for pair, axis in zip(pairs, axes)]
    hand, table = lax.optimization_barrier((hand, table))
    kept = tile_products(2, STREAMS, table, x, tiles, rows)
    sides = turn_sums(kept, got_own[0] + got_own[1], got_last[0] + got_last[1])
    return dense(spread(sides), weight, bias)


def solution(mesh):
    fine = Mesh(mesh.devices.reshape(-1, 2, SIDE, SIDE), ("y", "core", "x", "z"))
    grid = (("y", "core"), ("x", "z"))
    flat = ("y", "core", "x", "z")
    in_specs = (
        P(flat, None),
        P(flat),
        P(*grid, None, None, None),
        P(*grid, None, None),
        P(*grid),
        P(),
        P(),
    )
    return jax.shard_map(
        body, mesh=fine, in_specs=in_specs, out_specs=P(flat, None), check_vma=False
    )
```

```python
import functools

import jax
import jax.numpy as jnp
from jax import lax
from jax.experimental import pallas as pl
from jax.experimental.pallas import tpu as pltpu
from jax.sharding import Mesh
from jax.sharding import PartitionSpec as P

EXTRA = 8
PICK = 1024
UNROLL = 16
SLOTS = 6
STREAMS = 4
PAIR = 2
SIDE = 4
LANES = 128
F32 = jnp.float32
BF16 = jnp.bfloat16


def iota(shape, axis):
    return lax.broadcasted_iota(jnp.int32, shape, axis)


def log2(size):
    assert size & (size - 1) == 0
    return size.bit_length() - 1


def params(mib, **rest):
    return pltpu.CompilerParams(vmem_limit_bytes=mib << 20, **rest)


VMEM = pl.BlockSpec(memory_space=pltpu.VMEM)
SMEM = pl.BlockSpec(memory_space=pltpu.SMEM)
HBM = pl.BlockSpec(memory_space=pltpu.HBM)


def pack_kernel(
    grid_rows,
    grid_cols,
    capacity,
    index_hbm,
    rows_hbm,
    out_ref,
    index_ref,
    rows_ref,
    hits_ref,
    marks_ref,
    sems,
):
    local_rows, width = rows_ref.shape
    index_copy = pltpu.make_async_copy(index_hbm, index_ref, sems.at[0])
    index_copy.start()
    copy = pltpu.make_async_copy(rows_hbm, rows_ref, sems.at[1])
    copy.start()
    peers = grid_rows * grid_cols
    lanes = (LANES, 2 * LANES)
    earlier = jnp.where(iota(lanes, 0) < iota(lanes, 1), 1.0, 0.0).astype(BF16)
    rank_lane = iota((LANES, LANES), 0) & (capacity - 1)
    seen = jnp.zeros((peers, LANES), F32)
    zero = jnp.zeros((LANES, LANES), F32)
    places = []
    index_copy.wait()
    for block in range(local_rows // LANES):
        here = slice(block * LANES, (block + 1) * LANES)
        index = index_ref[block : block + 1, :]
        owner = index >> log2(local_rows)
        slot = index & (local_rows - 1)
        row = owner & (grid_rows - 1)
        peer = ((row & 1) * (grid_rows // 2) + (row >> 1)) * grid_cols + (owner >> log2(grid_rows))
        hit = jnp.where(iota((peers, LANES), 0) == peer, 1.0, 0.0)
        hits_ref[:, here] = hit.astype(BF16)
        counts = jnp.dot(hit.astype(BF16), earlier, preferred_element_type=F32)
        rank = jnp.sum((counts[:, :LANES] + seen) * hit, axis=0, keepdims=True).astype(jnp.int32)
        seen = seen + counts[:, LANES:]
        places.append(peer * capacity + rank)
        same = rank_lane == rank
        high = jnp.where(same, ((slot >> 7) + 1).astype(F32), zero)
        low = jnp.where(same, (slot & 127).astype(F32), zero)
        marks_ref[:LANES, here] = high.astype(BF16)
        marks_ref[LANES:, here] = low.astype(BF16)
    marks = lax.dot_general(
        hits_ref[...], marks_ref[...], (((1,), (1,)), ((), ())), preferred_element_type=F32
    )
    at = iota((peers, EXTRA, LANES), 1)
    none = jnp.zeros((peers, EXTRA, LANES), F32)
    extra = jnp.where(
        at == 0,
        marks[:, :LANES].reshape(peers, 1, LANES) + none,
        jnp.where(at == 1, marks[:, LANES:].reshape(peers, 1, LANES) + none, none),
    )
    out_ref[:, capacity:, :] = extra.astype(BF16)
    place = jnp.concatenate(places, axis=1)
    part = PICK // capacity
    copy.wait()

    def pick_rows(step, carry):
        pick = (iota((PICK, local_rows), 0) + step * PICK == place).astype(F32).astype(BF16)
        rows = jnp.dot(pick, rows_ref[...], preferred_element_type=F32).astype(BF16)
        out_ref[pl.ds(step * part, part), 0:capacity, :] = rows.reshape(part, capacity, width)
        return carry

    lax.fori_loop(0, peers * capacity // PICK, pick_rows, 0)


def pack_rows(index, rows, grid_rows, grid_cols, capacity):
    peers = grid_rows * grid_cols
    local_rows, width = rows.shape
    return pl.pallas_call(
        functools.partial(pack_kernel, grid_rows, grid_cols, capacity),
        out_shape=jax.ShapeDtypeStruct((peers, capacity + EXTRA, width), BF16),
        in_specs=[HBM] * 2,
        out_specs=VMEM,
        scratch_shapes=[
            pltpu.VMEM((local_rows // LANES, LANES), jnp.int32),
            pltpu.VMEM((local_rows, width), BF16),
            pltpu.VMEM((peers, local_rows), BF16),
            pltpu.VMEM((2 * LANES, local_rows), BF16),
            pltpu.SemaphoreType.DMA((2,)),
        ],
        compiler_params=params(60),
        name="pack_rows",
    )(index.reshape(-1, LANES), rows)


def place_kernel(in_ref, out_ref, slot_ref, rows_ref):
    peers, held, width = in_ref.shape
    capacity = held - EXTRA
    local_rows = out_ref.shape[0]
    per = LANES // capacity
    extra = in_ref[:, capacity:, :].astype(F32)
    high, low = extra[:, 0, :], extra[:, 1, :]
    slot_ref[...] = jnp.where(high > 0.5, (high - 1.0) * 128.0 + low, -1.0)
    rows_ref[...] = in_ref[:, 0:capacity, :].reshape(peers * capacity, width)
    which = iota((peers // per, LANES), 1) >> log2(capacity)
    slot = jnp.zeros((peers // per, LANES), F32)
    for i in range(per):
        slot = jnp.where(which == i, slot_ref[pl.ds(i, peers // per, stride=per), :], slot)
    slot = slot.astype(jnp.int32)
    slot = jnp.concatenate([slot[q : q + 1, :] for q in range(peers // per)], axis=1)

    def place_rows(step, carry):
        pick = (iota((PICK, peers * capacity), 0) + step * PICK == slot).astype(F32).astype(BF16)
        rows = jnp.dot(pick, rows_ref[...], preferred_element_type=F32)
        out_ref[pl.ds(pl.multiple_of(step * PICK, PICK), PICK), :] = rows.astype(BF16)
        return carry

    lax.fori_loop(0, local_rows // PICK, place_rows, 0)


def place_rows(got, local_rows):
    peers, held, width = got.shape
    return pl.pallas_call(
        place_kernel,
        out_shape=jax.ShapeDtypeStruct((local_rows, width), BF16),
        in_specs=[VMEM],
        out_specs=VMEM,
        scratch_shapes=[
            pltpu.VMEM((peers, LANES), F32),
            pltpu.VMEM((peers * (held - EXTRA), width), BF16),
        ],
        compiler_params=params(32),
        name="place_rows",
    )(got)


def tile_codes(index, me_x, me_z, me_y, me_core):
    row, col = index[0], index[1]
    d_y, d_core = (col >> 5) ^ me_y, ((col >> 4) & 1) ^ me_core
    col = ((d_y ^ (d_y >> 1)) << 5) | (d_core << 4) | (col & 15)
    tile = jnp.arange(index.shape[1], dtype=jnp.int32)
    dest, inner = row >> 4, row & 15
    stream, sub = inner >> 2, inner & 3
    d_x, d_z = (dest >> 2) ^ me_x, (dest & 3) ^ me_z
    first = jnp.where(stream < 2, d_x, d_z)
    second = jnp.where(stream < 2, d_z, d_x)
    near = jnp.where(stream & 1 == 0, 1, 3)
    place = stream * 16 + second * 4 + sub
    group = jnp.where(first == 0, 2, jnp.where(first == 2, 0, 1))
    place = place + jnp.where((group == 1) & (first != near), 64, 0)
    return (group << 25) | (tile << 15) | (place << 7) | col


def plan_kernel(count_ref, code_ref, table_ref):
    for group in range(3):
        table_ref[3, group] = 0

    def visit(step, carry):
        for sub in range(8):
            code = code_ref[step * 8 + sub]
            group = code >> 25
            at = table_ref[3, group]
            table_ref[group, at] = code
            table_ref[3, group] = at + 1
        return carry

    count = count_ref[0]
    full = count // 8
    lax.fori_loop(0, full, visit, 0)

    def visit_one(tile, carry):
        code = code_ref[tile]
        group = code >> 25
        at = table_ref[3, group]
        table_ref[group, at] = code
        table_ref[3, group] = at + 1
        return carry

    lax.fori_loop(full * 8, count, visit_one, 0)
    for group in range(3):
        for step in range(UNROLL):
            table_ref[group, table_ref[3, group] + step] = 128 << 7


def plan_tiles(count, codes):
    return pl.pallas_call(
        plan_kernel,
        out_shape=jax.ShapeDtypeStruct((4, codes.shape[0] + UNROLL), jnp.int32),
        in_specs=[SMEM] * 2,
        out_specs=SMEM,
        name="plan_tiles",
    )(count, codes)


def tile_kernel(group, arrays, pieces, table_ref, *refs):
    x_refs, tiles_ref, refs = refs[:pieces], refs[pieces], refs[pieces + 1 :]
    out_refs, (held, totals, sems) = refs[:arrays], refs[-3:]
    x_ref = x_refs[0] if pieces == 1 else refs[arrays]
    edge = held.shape[2]
    steps = (table_ref[3, group] + UNROLL - 1) // UNROLL

    def fetch(step):
        lane = lax.rem(step, SLOTS)
        for sub in range(UNROLL):
            tile = (table_ref[group, step * UNROLL + sub] >> 15) & 1023
            pltpu.make_async_copy(tiles_ref.at[tile], held.at[lane, sub], sems.at[lane]).start()

    for ahead in range(SLOTS - 1):

        @pl.when(ahead < steps)
        def _():
            fetch(ahead)

    totals[...] = jnp.zeros_like(totals)
    if pieces > 1:
        start = 0
        for piece in x_refs:
            x_ref[start : start + piece.shape[0], :] = piece[...]
            start += piece.shape[0]

    def add_tiles(step, carry):
        @pl.when(step + SLOTS - 1 < steps)
        def _():
            fetch(step + SLOTS - 1)

        lane = lax.rem(step, SLOTS)
        pltpu.make_async_copy(tiles_ref.at[pl.ds(0, UNROLL)], held.at[lane], sems.at[lane]).wait()
        for sub in range(UNROLL):
            code = table_ref[group, step * UNROLL + sub]
            row = jnp.minimum((code >> 7) & 255, totals.shape[0] // edge - 1)
            col = code & 127
            product = jnp.dot(
                held[lane, sub],
                x_ref[pl.ds(pl.multiple_of(col * edge, edge), edge), :],
                preferred_element_type=F32,
            )
            totals[pl.ds(pl.multiple_of(row * edge, edge), edge), :] += product
        return carry

    lax.fori_loop(0, steps, add_tiles, 0)
    rows = out_refs[0].shape[0]
    for array, out_ref in enumerate(out_refs):
        out_ref[...] = totals[array * rows : (array + 1) * rows, :].astype(BF16)


def tile_products(group, arrays, table, pieces, tiles, rows):
    _, edge, _ = tiles.shape
    width = pieces[0].shape[1]
    outs = [jax.ShapeDtypeStruct((rows, width), BF16)] * arrays
    if len(pieces) > 1:
        outs.append(jax.ShapeDtypeStruct((sum(p.shape[0] for p in pieces), width), BF16))
    return pl.pallas_call(
        functools.partial(tile_kernel, group, arrays, len(pieces)),
        out_shape=outs,
        in_specs=[SMEM] + [VMEM] * len(pieces) + [HBM],
        out_specs=[VMEM] * len(outs),
        scratch_shapes=[
            pltpu.VMEM((SLOTS, UNROLL, edge, edge), BF16),
            pltpu.VMEM((arrays * rows + edge, width), F32),
            pltpu.SemaphoreType.DMA((SLOTS,)),
        ],
        compiler_params=params(32),
        cost_estimate=pl.CostEstimate(
            flops=5_000_000_000 * arrays, bytes_accessed=5_000_000 * arrays, transcendentals=0
        ),
        name="tile_products",
    )(table, *pieces, tiles)


def wide(ref, start, rows):
    return ref[start : start + rows, :].astype(F32)


def forward_kernel(*refs):
    for stream in range(STREAMS):
        kept, got, out = refs[2 * stream], refs[2 * stream + 1], refs[2 * STREAMS + stream]
        out[...] = (kept[...].astype(F32) + got[...].astype(F32)).astype(BF16)


def forward_sums(kept, got):
    pairs = [array for pair in zip(kept, got) for array in pair]
    return pl.pallas_call(
        forward_kernel,
        out_shape=[jax.ShapeDtypeStruct(kept[0].shape, BF16)] * STREAMS,
        in_specs=[VMEM] * len(pairs),
        out_specs=[VMEM] * STREAMS,
        compiler_params=params(32),
        name="forward_sums",
    )(*pairs)


def turn_kernel(*refs):
    outs = refs[3 * STREAMS :]
    for stream in range(STREAMS):
        kept, got, last = refs[3 * stream : 3 * stream + 3]
        rows = last.shape[0] // SIDE
        at = stream % PAIR * rows
        for delta in range(SIDE):
            start = delta * rows
            total = wide(kept, start, rows) + wide(got, start, rows) + wide(last, start, rows)
            out = outs[stream // PAIR * SIDE + delta]
            out[at : at + rows, :] = total.astype(out.dtype)


def turn_sums(kept, got, last):
    ins = [array for three in zip(kept, got, last) for array in three]
    rows, width = last[0].shape
    shape = (PAIR * rows // SIDE, width)
    outs = [jax.ShapeDtypeStruct(shape, F32)] + [jax.ShapeDtypeStruct(shape, BF16)] * (SIDE - 1)
    done = pl.pallas_call(
        turn_kernel,
        out_shape=outs * 2,
        in_specs=[VMEM] * len(ins),
        out_specs=[VMEM] * (2 * SIDE),
        compiler_params=params(32),
        name="turn_sums",
    )(*ins)
    return done[:SIDE], done[SIDE:]


def dense_kernel(*refs):
    weight_ref, bias_ref, out_ref = refs[2 * SIDE :]
    for side in range(2):
        own, *got = refs[side * SIDE : (side + 1) * SIDE]
        rows = own.shape[0]
        total = own[...]
        for ref in got:
            total += ref[...].astype(F32)
        hidden = jnp.dot(total.astype(BF16), weight_ref[...], preferred_element_type=F32)
        hidden = jnp.maximum(hidden + bias_ref[...], 0.0)
        out_ref[side * rows : (side + 1) * rows, :] = hidden.astype(BF16)


def dense(terms, weight, bias):
    return pl.pallas_call(
        dense_kernel,
        out_shape=jax.ShapeDtypeStruct((2 * terms[0].shape[0], weight.shape[1]), BF16),
        in_specs=[VMEM] * (len(terms) + 2),
        out_specs=VMEM,
        compiler_params=params(32),
        name="dense",
    )(*terms, weight, bias.reshape(1, -1))


def gather_pieces(own):
    def over(array, axis, bit):
        pairs = [(c, c ^ bit) for c in range(lax.axis_size(axis))]
        return lax.ppermute(array, axis, pairs)

    half = own.shape[0] // 2
    one, three = over(own, "y", 1), over(own, "y", 3)
    other = over(own, "core", 1)
    far = [over(one[:half], "y", 3), over(three[half:], "y", 1)]
    near = [over(piece, "core", 1) for piece in (one, three)]
    return [own, other, one, near[0], three, near[1], *far, *(over(p, "core", 1) for p in far)]


def swap(arrays, axis, first):
    return [
        lax.ppermute(array, axis, [(c, c ^ bit) for c in range(SIDE)])
        for array, bit in zip(arrays, (1, 3) if first else (3, 1))
    ]


def spread(sides):
    got = [list(side) for side in sides]
    for bit in (1, 2, 3):
        for side, axis in enumerate(("z", "x")):
            got[side][bit] = lax.ppermute(
                sides[side][bit], axis, [(c, c ^ bit) for c in range(SIDE)]
            )
    return got[0] + got[1]


def body(features, new_index, tile_values, tile_index, tile_count, weight, bias):
    grid_rows = lax.axis_size("y") * lax.axis_size("core")
    grid_cols = lax.axis_size("x") * lax.axis_size("z")
    local_rows = features.shape[0]
    everyone = ("core", "y", "x", "z")
    capacity = 2 * local_rows // (grid_rows * grid_cols)
    tiles = tile_values[0, 0]
    row_tiles = local_rows * grid_cols // tiles.shape[1]
    assert row_tiles == 256 and grid_cols == SIDE * SIDE

    codes = tile_codes(
        tile_index[0, 0], *(lax.axis_index(axis) for axis in ("x", "z", "y", "core"))
    )
    packed = pack_rows(new_index, features, grid_rows, grid_cols, capacity)
    got = lax.all_to_all(packed, everyone, split_axis=0, concat_axis=0, tiled=True)
    table = plan_tiles(tile_count.reshape(1), codes)
    got, table = lax.optimization_barrier((got, table))
    moved_rows = place_rows(got, local_rows)
    pieces = gather_pieces(moved_rows)

    rows = local_rows * grid_cols // 16
    axes = ("x", "z")
    pairs = (slice(0, PAIR), slice(PAIR, STREAMS))
    *sent_on, x = tile_products(0, STREAMS, table, pieces, tiles, rows)
    got_on = [swap(sent_on[pair], axis, True) for pair, axis in zip(pairs, axes)]
    both = tile_products(1, 2 * STREAMS, table, [x], tiles, rows)
    got_own = [swap(both[pair], axis, True) for pair, axis in zip(pairs, axes)]
    hand = forward_sums(both[STREAMS:], got_on[0] + got_on[1])
    got_last = [swap(hand[pair], axis, False) for pair, axis in zip(pairs, axes)]
    hand, table = lax.optimization_barrier((hand, table))
    kept = tile_products(2, STREAMS, table, [x], tiles, rows)
    sides = turn_sums(kept, got_own[0] + got_own[1], got_last[0] + got_last[1])
    return dense(spread(sides), weight, bias)


def solution(mesh):
    fine = Mesh(mesh.devices.reshape(-1, 2, SIDE, SIDE), ("y", "core", "x", "z"))
    grid = (("y", "core"), ("x", "z"))
    flat = ("y", "core", "x", "z")
    in_specs = (
        P(flat, None),
        P(flat),
        P(*grid, None, None, None),
        P(*grid, None, None),
        P(*grid),
        P(),
        P(),
    )
    return jax.shard_map(
        body, mesh=fine, in_specs=in_specs, out_specs=P(flat, None), check_vma=False
    )
```

```python
import functools

import jax
import jax.numpy as jnp
from jax import lax
from jax.experimental import pallas as pl
from jax.experimental.pallas import tpu as pltpu
from jax.sharding import Mesh
from jax.sharding import PartitionSpec as P

EXTRA = 8
PICK = 1024
UNROLL = 16
SLOTS = 6
STREAMS = 4
PAIR = 2
SIDE = 4
LANES = 128
F32 = jnp.float32
BF16 = jnp.bfloat16


def iota(shape, axis):
    return lax.broadcasted_iota(jnp.int32, shape, axis)


def log2(size):
    assert size & (size - 1) == 0
    return size.bit_length() - 1


def params(mib, **rest):
    return pltpu.CompilerParams(vmem_limit_bytes=mib << 20, **rest)


VMEM = pl.BlockSpec(memory_space=pltpu.VMEM)
SMEM = pl.BlockSpec(memory_space=pltpu.SMEM)
HBM = pl.BlockSpec(memory_space=pltpu.HBM)


def pack_kernel(
    grid_rows,
    grid_cols,
    capacity,
    index_hbm,
    rows_hbm,
    out_ref,
    index_ref,
    rows_ref,
    hits_ref,
    marks_ref,
    sems,
):
    local_rows, width = rows_ref.shape
    index_copy = pltpu.make_async_copy(index_hbm, index_ref, sems.at[0])
    index_copy.start()
    copy = pltpu.make_async_copy(rows_hbm, rows_ref, sems.at[1])
    copy.start()
    peers = grid_rows * grid_cols
    lanes = (LANES, 2 * LANES)
    earlier = jnp.where(iota(lanes, 0) < iota(lanes, 1), 1.0, 0.0).astype(BF16)
    rank_lane = iota((LANES, LANES), 0) & (capacity - 1)
    seen = jnp.zeros((peers, LANES), F32)
    zero = jnp.zeros((LANES, LANES), F32)
    places = []
    index_copy.wait()
    for block in range(local_rows // LANES):
        here = slice(block * LANES, (block + 1) * LANES)
        index = index_ref[block : block + 1, :]
        owner = index >> log2(local_rows)
        slot = index & (local_rows - 1)
        row = owner & (grid_rows - 1)
        peer = ((row & 1) * (grid_rows // 2) + (row >> 1)) * grid_cols + (owner >> log2(grid_rows))
        hit = jnp.where(iota((peers, LANES), 0) == peer, 1.0, 0.0)
        hits_ref[:, here] = hit.astype(BF16)
        counts = jnp.dot(hit.astype(BF16), earlier, preferred_element_type=F32)
        rank = jnp.sum((counts[:, :LANES] + seen) * hit, axis=0, keepdims=True).astype(jnp.int32)
        seen = seen + counts[:, LANES:]
        places.append(peer * capacity + rank)
        same = rank_lane == rank
        high = jnp.where(same, ((slot >> 7) + 1).astype(F32), zero)
        low = jnp.where(same, (slot & 127).astype(F32), zero)
        marks_ref[:LANES, here] = high.astype(BF16)
        marks_ref[LANES:, here] = low.astype(BF16)
    marks = lax.dot_general(
        hits_ref[...], marks_ref[...], (((1,), (1,)), ((), ())), preferred_element_type=F32
    )
    at = iota((peers, EXTRA, LANES), 1)
    none = jnp.zeros((peers, EXTRA, LANES), F32)
    extra = jnp.where(
        at == 0,
        marks[:, :LANES].reshape(peers, 1, LANES) + none,
        jnp.where(at == 1, marks[:, LANES:].reshape(peers, 1, LANES) + none, none),
    )
    out_ref[:, capacity:, :] = extra.astype(BF16)
    place = jnp.concatenate(places, axis=1)
    part = PICK // capacity
    copy.wait()

    def pick_rows(step, carry):
        pick = (iota((PICK, local_rows), 0) + step * PICK == place).astype(F32).astype(BF16)
        rows = jnp.dot(pick, rows_ref[...], preferred_element_type=F32).astype(BF16)
        out_ref[pl.ds(step * part, part), 0:capacity, :] = rows.reshape(part, capacity, width)
        return carry

    lax.fori_loop(0, peers * capacity // PICK, pick_rows, 0)


def pack_rows(index, rows, grid_rows, grid_cols, capacity):
    peers = grid_rows * grid_cols
    local_rows, width = rows.shape
    return pl.pallas_call(
        functools.partial(pack_kernel, grid_rows, grid_cols, capacity),
        out_shape=jax.ShapeDtypeStruct((peers, capacity + EXTRA, width), BF16),
        in_specs=[HBM] * 2,
        out_specs=VMEM,
        scratch_shapes=[
            pltpu.VMEM((local_rows // LANES, LANES), jnp.int32),
            pltpu.VMEM((local_rows, width), BF16),
            pltpu.VMEM((peers, local_rows), BF16),
            pltpu.VMEM((2 * LANES, local_rows), BF16),
            pltpu.SemaphoreType.DMA((2,)),
        ],
        compiler_params=params(60),
        name="pack_rows",
    )(index.reshape(-1, LANES), rows)


def place_kernel(in_ref, out_ref, slot_ref, rows_ref):
    peers, held, width = in_ref.shape
    capacity = held - EXTRA
    local_rows = out_ref.shape[0]
    per = LANES // capacity
    extra = in_ref[:, capacity:, :].astype(F32)
    high, low = extra[:, 0, :], extra[:, 1, :]
    slot_ref[...] = jnp.where(high > 0.5, (high - 1.0) * 128.0 + low, -1.0)
    rows_ref[...] = in_ref[:, 0:capacity, :].reshape(peers * capacity, width)
    which = iota((peers // per, LANES), 1) >> log2(capacity)
    slot = jnp.zeros((peers // per, LANES), F32)
    for i in range(per):
        slot = jnp.where(which == i, slot_ref[pl.ds(i, peers // per, stride=per), :], slot)
    slot = slot.astype(jnp.int32)
    slot = jnp.concatenate([slot[q : q + 1, :] for q in range(peers // per)], axis=1)

    def place_rows(step, carry):
        pick = (iota((PICK, peers * capacity), 0) + step * PICK == slot).astype(F32).astype(BF16)
        rows = jnp.dot(pick, rows_ref[...], preferred_element_type=F32)
        out_ref[pl.ds(pl.multiple_of(step * PICK, PICK), PICK), :] = rows.astype(BF16)
        return carry

    lax.fori_loop(0, local_rows // PICK, place_rows, 0)


def place_rows(got, local_rows):
    peers, held, width = got.shape
    return pl.pallas_call(
        place_kernel,
        out_shape=jax.ShapeDtypeStruct((local_rows, width), BF16),
        in_specs=[VMEM],
        out_specs=VMEM,
        scratch_shapes=[
            pltpu.VMEM((peers, LANES), F32),
            pltpu.VMEM((peers * (held - EXTRA), width), BF16),
        ],
        compiler_params=params(32),
        name="place_rows",
    )(got)


def tile_codes(index, me_x, me_z, me_y, me_core):
    row, col = index[0], index[1]
    owner = (((col >> 5) ^ me_y) << 1) | (((col >> 4) & 1) ^ me_core)
    block = (0x53764210 >> (4 * owner)) & 7
    col = (block << 4) | (col & 15)
    tile = jnp.arange(index.shape[1], dtype=jnp.int32)
    dest, inner = row >> 4, row & 15
    stream, sub = inner >> 2, inner & 3
    d_x, d_z = (dest >> 2) ^ me_x, (dest & 3) ^ me_z
    first = jnp.where(stream < 2, d_x, d_z)
    second = jnp.where(stream < 2, d_z, d_x)
    near = jnp.where(stream & 1 == 0, 1, 3)
    place = stream * 16 + second * 4 + sub
    group = jnp.where(first == 0, 2, jnp.where(first == 2, 0, 1))
    place = place + jnp.where((group == 1) & (first != near), 64, 0)
    group = jnp.where((group == 0) & (block >= 6), 3, group)
    return (group << 25) | (tile << 15) | (place << 7) | col


def plan_kernel(count_ref, code_ref, table_ref):
    for group in range(4):
        table_ref[4, group] = 0

    def visit(step, carry):
        for sub in range(8):
            code = code_ref[step * 8 + sub]
            group = code >> 25
            at = table_ref[4, group]
            table_ref[group, at] = code
            table_ref[4, group] = at + 1
        return carry

    count = count_ref[0]
    full = count // 8
    lax.fori_loop(0, full, visit, 0)

    def visit_one(tile, carry):
        code = code_ref[tile]
        group = code >> 25
        at = table_ref[4, group]
        table_ref[group, at] = code
        table_ref[4, group] = at + 1
        return carry

    lax.fori_loop(full * 8, count, visit_one, 0)
    for group in range(4):
        for step in range(UNROLL):
            table_ref[group, table_ref[4, group] + step] = 128 << 7


def plan_tiles(count, codes):
    return pl.pallas_call(
        plan_kernel,
        out_shape=jax.ShapeDtypeStruct((5, codes.shape[0] + UNROLL), jnp.int32),
        in_specs=[SMEM] * 2,
        out_specs=SMEM,
        name="plan_tiles",
    )(count, codes)


def add_list(group, table_ref, x_ref, tiles_ref, held, totals, sems, prepare):
    edge = held.shape[2]
    steps = (table_ref[4, group] + UNROLL - 1) // UNROLL

    def fetch(step):
        lane = lax.rem(step, SLOTS)
        for sub in range(UNROLL):
            tile = (table_ref[group, step * UNROLL + sub] >> 15) & 1023
            pltpu.make_async_copy(tiles_ref.at[tile], held.at[lane, sub], sems.at[lane]).start()

    for ahead in range(SLOTS - 1):

        @pl.when(ahead < steps)
        def _():
            fetch(ahead)

    prepare()

    def add_tiles(step, carry):
        @pl.when(step + SLOTS - 1 < steps)
        def _():
            fetch(step + SLOTS - 1)

        lane = lax.rem(step, SLOTS)
        pltpu.make_async_copy(tiles_ref.at[pl.ds(0, UNROLL)], held.at[lane], sems.at[lane]).wait()
        for sub in range(UNROLL):
            code = table_ref[group, step * UNROLL + sub]
            row = jnp.minimum((code >> 7) & 255, totals.shape[0] // edge - 1)
            col = code & 127
            product = jnp.dot(
                held[lane, sub],
                x_ref[pl.ds(pl.multiple_of(col * edge, edge), edge), :],
                preferred_element_type=F32,
            )
            totals[pl.ds(pl.multiple_of(row * edge, edge), edge), :] += product
        return carry

    lax.fori_loop(0, steps, add_tiles, 0)


def write_totals(totals, out_refs):
    rows = out_refs[0].shape[0]
    for array, out_ref in enumerate(out_refs):
        out_ref[...] = totals[array * rows : (array + 1) * rows, :].astype(BF16)


def join(pieces, out_ref, start):
    for piece in pieces:
        out_ref[start : start + piece.shape[0], :] = piece[...]
        start += piece.shape[0]


def early_kernel(group, pieces, table_ref, *refs):
    x_refs, (tiles_ref, x_out, totals, held, sems) = refs[:pieces], refs[pieces:]

    def prepare():
        totals[...] = jnp.zeros_like(totals)
        join(x_refs, x_out, 0)

    add_list(group, table_ref, x_out, tiles_ref, held, totals, sems, prepare)


def late_kernel(group, arrays, pieces, table_ref, *refs):
    x_refs, (tiles_ref, x_in, totals_in, x_out, totals), refs = (
        refs[:pieces],
        refs[pieces : pieces + 5],
        refs[pieces + 5 :],
    )
    out_refs, (held, sems) = refs[:arrays], refs[arrays:]
    rows = sum(piece.shape[0] for piece in x_refs)

    def prepare():
        join(x_refs, x_out, x_out.shape[0] - rows)

    add_list(group, table_ref, x_out, tiles_ref, held, totals, sems, prepare)
    write_totals(totals, out_refs)


def tile_kernel(group, arrays, table_ref, x_ref, tiles_ref, *refs):
    out_refs, (totals, held, sems) = refs[:arrays], refs[arrays:]

    def prepare():
        totals[...] = jnp.zeros_like(totals)

    add_list(group, table_ref, x_ref, tiles_ref, held, totals, sems, prepare)
    write_totals(totals, out_refs)


def tile_scratch(tiles):
    _, edge, _ = tiles.shape
    return [pltpu.VMEM((SLOTS, UNROLL, edge, edge), BF16), pltpu.SemaphoreType.DMA((SLOTS,))]


def work(arrays):
    return pl.CostEstimate(
        flops=5_000_000_000 * arrays, bytes_accessed=5_000_000 * arrays, transcendentals=0
    )


def tile_products(group, arrays, table, x, tiles, rows):
    edge, width = tiles.shape[1], x.shape[1]
    return pl.pallas_call(
        functools.partial(tile_kernel, group, arrays),
        out_shape=[jax.ShapeDtypeStruct((rows, width), BF16)] * arrays,
        in_specs=[SMEM, VMEM, HBM],
        out_specs=[VMEM] * arrays,
        scratch_shapes=[pltpu.VMEM((arrays * rows + edge, width), F32), *tile_scratch(tiles)],
        compiler_params=params(32),
        cost_estimate=work(arrays),
        name="tile_products",
    )(table, x, tiles)


def early_products(group, arrays, table, pieces, x_rows, tiles, rows):
    edge, width = tiles.shape[1], pieces[0].shape[1]
    return pl.pallas_call(
        functools.partial(early_kernel, group, len(pieces)),
        out_shape=[
            jax.ShapeDtypeStruct((x_rows, width), BF16),
            jax.ShapeDtypeStruct((arrays * rows + edge, width), F32),
        ],
        in_specs=[SMEM] + [VMEM] * len(pieces) + [HBM],
        out_specs=[VMEM] * 2,
        scratch_shapes=tile_scratch(tiles),
        compiler_params=params(32),
        cost_estimate=work(1),
        name="early_products",
    )(table, *pieces, tiles)


def late_products(group, arrays, table, pieces, x, totals, tiles, rows):
    width = x.shape[1]
    at = len(pieces) + 2
    return pl.pallas_call(
        functools.partial(late_kernel, group, arrays, len(pieces)),
        out_shape=[
            jax.ShapeDtypeStruct(x.shape, x.dtype),
            jax.ShapeDtypeStruct(totals.shape, totals.dtype),
        ]
        + [jax.ShapeDtypeStruct((rows, width), BF16)] * arrays,
        in_specs=[SMEM] + [VMEM] * len(pieces) + [HBM, VMEM, VMEM],
        out_specs=[VMEM] * (2 + arrays),
        scratch_shapes=tile_scratch(tiles),
        input_output_aliases={at: 0, at + 1: 1},
        compiler_params=params(32),
        cost_estimate=work(1),
        name="late_products",
    )(table, *pieces, tiles, x, totals)


def wide(ref, start, rows):
    return ref[start : start + rows, :].astype(F32)


def forward_kernel(*refs):
    for stream in range(STREAMS):
        kept, got, out = refs[2 * stream], refs[2 * stream + 1], refs[2 * STREAMS + stream]
        out[...] = (kept[...].astype(F32) + got[...].astype(F32)).astype(BF16)


def forward_sums(kept, got):
    pairs = [array for pair in zip(kept, got) for array in pair]
    return pl.pallas_call(
        forward_kernel,
        out_shape=[jax.ShapeDtypeStruct(kept[0].shape, BF16)] * STREAMS,
        in_specs=[VMEM] * len(pairs),
        out_specs=[VMEM] * STREAMS,
        compiler_params=params(32),
        name="forward_sums",
    )(*pairs)


def turn_kernel(*refs):
    outs = refs[3 * PAIR :]
    for stream in range(PAIR):
        kept, got, last = refs[3 * stream : 3 * stream + 3]
        rows = last.shape[0] // SIDE
        at = stream * rows
        for delta in range(SIDE):
            start = delta * rows
            total = wide(kept, start, rows) + wide(got, start, rows) + wide(last, start, rows)
            out = outs[delta]
            out[at : at + rows, :] = total.astype(out.dtype)


def turn_sums(kept, got, last):
    ins = [array for three in zip(kept, got, last) for array in three]
    rows, width = last[0].shape
    shape = (PAIR * rows // SIDE, width)
    outs = [jax.ShapeDtypeStruct(shape, F32)] + [jax.ShapeDtypeStruct(shape, BF16)] * (SIDE - 1)
    return pl.pallas_call(
        turn_kernel,
        out_shape=outs,
        in_specs=[VMEM] * len(ins),
        out_specs=[VMEM] * SIDE,
        compiler_params=params(32),
        name="turn_sums",
    )(*ins)


def dense_kernel(*refs):
    weight_ref, bias_ref, out_ref = refs[2 * SIDE :]
    for side in range(2):
        own, *got = refs[side * SIDE : (side + 1) * SIDE]
        rows = own.shape[0]
        total = own[...]
        for ref in got:
            total += ref[...].astype(F32)
        hidden = jnp.dot(total.astype(BF16), weight_ref[...], preferred_element_type=F32)
        hidden = jnp.maximum(hidden + bias_ref[...], 0.0)
        out_ref[side * rows : (side + 1) * rows, :] = hidden.astype(BF16)


def dense(terms, weight, bias):
    return pl.pallas_call(
        dense_kernel,
        out_shape=jax.ShapeDtypeStruct((2 * terms[0].shape[0], weight.shape[1]), BF16),
        in_specs=[VMEM] * (len(terms) + 2),
        out_specs=VMEM,
        compiler_params=params(32),
        name="dense",
    )(*terms, weight, bias.reshape(1, -1))


def over(array, axis, bit):
    pairs = [(c, c ^ bit) for c in range(lax.axis_size(axis))]
    return lax.ppermute(array, axis, pairs)


def gather_first(own):
    half = own.shape[0] // 2
    one, three = over(own, "y", 1), over(own, "y", 3)
    other = over(own, "core", 1)
    far = [over(one[:half], "y", 3), over(three[half:], "y", 1)]
    near = [over(piece, "core", 1) for piece in (one, three)]
    return [own, other, one, three, *near], far


def swap(arrays, axis, first):
    return [
        lax.ppermute(array, axis, [(c, c ^ bit) for c in range(SIDE)])
        for array, bit in zip(arrays, (1, 3) if first else (3, 1))
    ]


def spread(sums, axis):
    mine, *send = sums
    got = [
        lax.ppermute(array, axis, [(c, c ^ bit) for c in range(SIDE)])
        for bit, array in enumerate(send, 1)
    ]
    return [mine, *got]


def body(features, new_index, tile_values, tile_index, tile_count, weight, bias):
    grid_rows = lax.axis_size("y") * lax.axis_size("core")
    grid_cols = lax.axis_size("x") * lax.axis_size("z")
    local_rows = features.shape[0]
    everyone = ("core", "y", "x", "z")
    capacity = 2 * local_rows // (grid_rows * grid_cols)
    tiles = tile_values[0, 0]
    row_tiles = local_rows * grid_cols // tiles.shape[1]
    assert row_tiles == 256 and grid_cols == SIDE * SIDE

    codes = tile_codes(
        tile_index[0, 0], *(lax.axis_index(axis) for axis in ("x", "z", "y", "core"))
    )
    packed = pack_rows(new_index, features, grid_rows, grid_cols, capacity)
    got = lax.all_to_all(packed, everyone, split_axis=0, concat_axis=0, tiled=True)
    table = plan_tiles(tile_count.reshape(1), codes)
    got, table = lax.optimization_barrier((got, table))
    moved_rows = place_rows(got, local_rows)
    early, far = gather_first(moved_rows)

    rows = local_rows * grid_cols // 16
    axes = ("x", "z")
    pairs = (slice(0, PAIR), slice(PAIR, STREAMS))
    x_rows = local_rows * grid_rows
    x, totals = early_products(0, STREAMS, table, early, x_rows, tiles, rows)
    far, x, totals = lax.optimization_barrier((far, x, totals))
    late = [*far, *(over(piece, "core", 1) for piece in far)]
    x, _, *sent_on = late_products(3, STREAMS, table, late, x, totals, tiles, rows)
    got_on = [swap(sent_on[pair], axis, True) for pair, axis in zip(pairs, axes)]
    both = tile_products(1, 2 * STREAMS, table, x, tiles, rows)
    got_own = [swap(both[pair], axis, True) for pair, axis in zip(pairs, axes)]
    hand = forward_sums(both[STREAMS:], got_on[0] + got_on[1])
    got_last = [swap(hand[pair], axis, False) for pair, axis in zip(pairs, axes)]
    hand, table, got_own = lax.optimization_barrier((hand, table, got_own))
    kept = tile_products(2, STREAMS, table, x, tiles, rows)
    first = spread(turn_sums(kept[pairs[0]], got_own[0], got_last[0]), "z")
    second = spread(turn_sums(kept[pairs[1]], got_own[1], got_last[1]), "x")
    return dense(first + second, weight, bias)


def solution(mesh):
    fine = Mesh(mesh.devices.reshape(-1, 2, SIDE, SIDE), ("y", "core", "x", "z"))
    grid = (("y", "core"), ("x", "z"))
    flat = ("y", "core", "x", "z")
    in_specs = (
        P(flat, None),
        P(flat),
        P(*grid, None, None, None),
        P(*grid, None, None),
        P(*grid),
        P(),
        P(),
    )
    return jax.shard_map(
        body, mesh=fine, in_specs=in_specs, out_specs=P(flat, None), check_vma=False
    )
```

```python
import functools

import jax
import jax.numpy as jnp
from jax import lax
from jax.experimental import pallas as pl
from jax.experimental.pallas import tpu as pltpu
from jax.sharding import Mesh
from jax.sharding import PartitionSpec as P

EXTRA = 8
PICK = 1024
UNROLL = 20
SLOTS = 8
STREAMS = 4
PAIR = 2
SIDE = 4
LANES = 128
F32 = jnp.float32
BF16 = jnp.bfloat16


def iota(shape, axis):
    return lax.broadcasted_iota(jnp.int32, shape, axis)


def log2(size):
    assert size & (size - 1) == 0
    return size.bit_length() - 1


def params(mib, **rest):
    return pltpu.CompilerParams(vmem_limit_bytes=mib << 20, **rest)


VMEM = pl.BlockSpec(memory_space=pltpu.VMEM)
SMEM = pl.BlockSpec(memory_space=pltpu.SMEM)
HBM = pl.BlockSpec(memory_space=pltpu.HBM)


def pack_kernel(
    grid_rows,
    grid_cols,
    capacity,
    index_hbm,
    rows_hbm,
    out_ref,
    index_ref,
    rows_ref,
    hits_ref,
    marks_ref,
    sems,
):
    local_rows, width = rows_ref.shape
    index_copy = pltpu.make_async_copy(index_hbm, index_ref, sems.at[0])
    index_copy.start()
    copy = pltpu.make_async_copy(rows_hbm, rows_ref, sems.at[1])
    copy.start()
    peers = grid_rows * grid_cols
    lanes = (LANES, 2 * LANES)
    earlier = jnp.where(iota(lanes, 0) < iota(lanes, 1), 1.0, 0.0).astype(BF16)
    rank_lane = iota((LANES, LANES), 0) & (capacity - 1)
    seen = jnp.zeros((peers, LANES), F32)
    zero = jnp.zeros((LANES, LANES), F32)
    places = []
    index_copy.wait()
    for block in range(local_rows // LANES):
        here = slice(block * LANES, (block + 1) * LANES)
        index = index_ref[block : block + 1, :]
        owner = index >> log2(local_rows)
        slot = index & (local_rows - 1)
        row = owner & (grid_rows - 1)
        peer = ((row & 1) * (grid_rows // 2) + (row >> 1)) * grid_cols + (owner >> log2(grid_rows))
        hit = jnp.where(iota((peers, LANES), 0) == peer, 1.0, 0.0)
        hits_ref[:, here] = hit.astype(BF16)
        counts = jnp.dot(hit.astype(BF16), earlier, preferred_element_type=F32)
        rank = jnp.sum((counts[:, :LANES] + seen) * hit, axis=0, keepdims=True).astype(jnp.int32)
        seen = seen + counts[:, LANES:]
        places.append(peer * capacity + rank)
        same = rank_lane == rank
        high = jnp.where(same, ((slot >> 7) + 1).astype(F32), zero)
        low = jnp.where(same, (slot & 127).astype(F32), zero)
        marks_ref[:LANES, here] = high.astype(BF16)
        marks_ref[LANES:, here] = low.astype(BF16)
    marks = lax.dot_general(
        hits_ref[...], marks_ref[...], (((1,), (1,)), ((), ())), preferred_element_type=F32
    )
    at = iota((peers, EXTRA, LANES), 1)
    none = jnp.zeros((peers, EXTRA, LANES), F32)
    extra = jnp.where(
        at == 0,
        marks[:, :LANES].reshape(peers, 1, LANES) + none,
        jnp.where(at == 1, marks[:, LANES:].reshape(peers, 1, LANES) + none, none),
    )
    out_ref[:, capacity:, :] = extra.astype(BF16)
    place = jnp.concatenate(places, axis=1)
    part = PICK // capacity
    copy.wait()

    def pick_rows(step, carry):
        pick = (iota((PICK, local_rows), 0) + step * PICK == place).astype(F32).astype(BF16)
        rows = jnp.dot(pick, rows_ref[...], preferred_element_type=F32).astype(BF16)
        out_ref[pl.ds(step * part, part), 0:capacity, :] = rows.reshape(part, capacity, width)
        return carry

    lax.fori_loop(0, peers * capacity // PICK, pick_rows, 0)


def pack_rows(index, rows, grid_rows, grid_cols, capacity):
    peers = grid_rows * grid_cols
    local_rows, width = rows.shape
    return pl.pallas_call(
        functools.partial(pack_kernel, grid_rows, grid_cols, capacity),
        out_shape=jax.ShapeDtypeStruct((peers, capacity + EXTRA, width), BF16),
        in_specs=[HBM] * 2,
        out_specs=VMEM,
        scratch_shapes=[
            pltpu.VMEM((local_rows // LANES, LANES), jnp.int32),
            pltpu.VMEM((local_rows, width), BF16),
            pltpu.VMEM((peers, local_rows), BF16),
            pltpu.VMEM((2 * LANES, local_rows), BF16),
            pltpu.SemaphoreType.DMA((2,)),
        ],
        compiler_params=params(60),
        name="pack_rows",
    )(index.reshape(-1, LANES), rows)


def place_kernel(first, in_ref, out_ref, slot_ref, rows_ref):
    peers, held, width = in_ref.shape
    capacity = held - EXTRA
    per = LANES // capacity
    extra = in_ref[:, capacity:, :].astype(F32)
    high, low = extra[:, 0, :], extra[:, 1, :]
    slot_ref[...] = jnp.where(high > 0.5, (high - 1.0) * 128.0 + low, -1.0)
    rows_ref[...] = in_ref[:, 0:capacity, :].reshape(peers * capacity, width)
    which = iota((peers // per, LANES), 1) >> log2(capacity)
    slot = jnp.zeros((peers // per, LANES), F32)
    for i in range(per):
        slot = jnp.where(which == i, slot_ref[pl.ds(i, peers // per, stride=per), :], slot)
    slot = slot.astype(jnp.int32)
    slot = jnp.concatenate([slot[q : q + 1, :] for q in range(peers // per)], axis=1)

    def place_rows(step, carry):
        pick = (iota((PICK, peers * capacity), 0) + (first + step * PICK) == slot).astype(F32).astype(BF16)
        rows = jnp.dot(pick, rows_ref[...], preferred_element_type=F32)
        out_ref[pl.ds(pl.multiple_of(step * PICK, PICK), PICK), :] = rows.astype(BF16)
        return carry

    lax.fori_loop(0, out_ref.shape[0] // PICK, place_rows, 0)


def place_rows(got, first, rows):
    peers, held, width = got.shape
    return pl.pallas_call(
        functools.partial(place_kernel, first),
        out_shape=jax.ShapeDtypeStruct((rows, width), BF16),
        in_specs=[VMEM],
        out_specs=VMEM,
        scratch_shapes=[
            pltpu.VMEM((peers, LANES), F32),
            pltpu.VMEM((peers * (held - EXTRA), width), BF16),
        ],
        compiler_params=params(32),
        name="place_rows",
    )(got)


def tile_codes(index, me_x, me_z, me_y, me_core):
    row, col = index[0], index[1]
    owner = (((col >> 5) ^ me_y) << 1) | (((col >> 4) & 1) ^ me_core)
    block = (0x53764210 >> (4 * owner)) & 7
    col = (block << 4) | (col & 15)
    tile = jnp.arange(index.shape[1], dtype=jnp.int32)
    dest, inner = row >> 4, row & 15
    stream, sub = inner >> 2, inner & 3
    d_x, d_z = (dest >> 2) ^ me_x, (dest & 3) ^ me_z
    first = jnp.where(stream < 2, d_x, d_z)
    second = jnp.where(stream < 2, d_z, d_x)
    near = jnp.where(stream & 1 == 0, 1, 3)
    place = stream * 16 + second * 4 + sub
    group = jnp.where(first == 0, 2, jnp.where(first == 2, 0, 1))
    place = place + jnp.where((group == 1) & (first != near), 64, 0)
    group = jnp.where((group == 0) & (block >= 6), 3, group)
    return (group << 25) | (tile << 15) | (place << 7) | col


def plan_kernel(count_ref, code_ref, table_ref):
    for group in range(4):
        table_ref[4, group] = 0

    def visit(step, carry):
        for sub in range(8):
            code = code_ref[step * 8 + sub]
            group = code >> 25
            at = table_ref[4, group]
            table_ref[group, at] = code
            table_ref[4, group] = at + 1
        return carry

    count = count_ref[0]
    full = count // 8
    lax.fori_loop(0, full, visit, 0)

    def visit_one(tile, carry):
        code = code_ref[tile]
        group = code >> 25
        at = table_ref[4, group]
        table_ref[group, at] = code
        table_ref[4, group] = at + 1
        return carry

    lax.fori_loop(full * 8, count, visit_one, 0)
    for group in range(4):
        for step in range(UNROLL):
            table_ref[group, table_ref[4, group] + step] = 128 << 7


def plan_tiles(count, codes):
    return pl.pallas_call(
        plan_kernel,
        out_shape=jax.ShapeDtypeStruct((5, codes.shape[0] + UNROLL), jnp.int32),
        in_specs=[SMEM] * 2,
        out_specs=SMEM,
        name="plan_tiles",
    )(count, codes)


def add_list(group, table_ref, x_ref, tiles_ref, held, totals, sems, prepare):
    edge = held.shape[2]
    steps = (table_ref[4, group] + UNROLL - 1) // UNROLL

    def fetch(step):
        lane = lax.rem(step, SLOTS)
        for sub in range(UNROLL):
            tile = (table_ref[group, step * UNROLL + sub] >> 15) & 1023
            pltpu.make_async_copy(tiles_ref.at[tile], held.at[lane, sub], sems.at[lane]).start()

    for ahead in range(SLOTS - 1):

        @pl.when(ahead < steps)
        def _():
            fetch(ahead)

    prepare()

    def add_tiles(step, carry):
        @pl.when(step + SLOTS - 1 < steps)
        def _():
            fetch(step + SLOTS - 1)

        lane = lax.rem(step, SLOTS)
        pltpu.make_async_copy(tiles_ref.at[pl.ds(0, UNROLL)], held.at[lane], sems.at[lane]).wait()
        for sub in range(UNROLL):
            code = table_ref[group, step * UNROLL + sub]
            row = jnp.minimum((code >> 7) & 255, totals.shape[0] // edge - 1)
            col = code & 127
            product = jnp.dot(
                held[lane, sub],
                x_ref[pl.ds(pl.multiple_of(col * edge, edge), edge), :],
                preferred_element_type=F32,
            )
            totals[pl.ds(pl.multiple_of(row * edge, edge), edge), :] += product
        return carry

    lax.fori_loop(0, steps, add_tiles, 0)


def write_totals(totals, out_refs):
    rows = out_refs[0].shape[0]
    for array, out_ref in enumerate(out_refs):
        out_ref[...] = totals[array * rows : (array + 1) * rows, :].astype(BF16)


def join(pieces, out_ref, start):
    for piece in pieces:
        out_ref[start : start + piece.shape[0], :] = piece[...]
        start += piece.shape[0]


def early_kernel(group, pieces, table_ref, *refs):
    x_refs, (tiles_ref, x_out, totals, held, sems) = refs[:pieces], refs[pieces:]

    def prepare():
        totals[...] = jnp.zeros_like(totals)
        join(x_refs, x_out, 0)

    add_list(group, table_ref, x_out, tiles_ref, held, totals, sems, prepare)


def late_kernel(group, arrays, pieces, table_ref, *refs):
    x_refs, (tiles_ref, x_in, totals_in, x_out, totals), refs = (
        refs[:pieces],
        refs[pieces : pieces + 5],
        refs[pieces + 5 :],
    )
    out_refs, (held, sems) = refs[:arrays], refs[arrays:]
    rows = sum(piece.shape[0] for piece in x_refs)

    def prepare():
        join(x_refs, x_out, x_out.shape[0] - rows)

    add_list(group, table_ref, x_out, tiles_ref, held, totals, sems, prepare)
    write_totals(totals, out_refs)


def tile_kernel(group, arrays, table_ref, x_ref, tiles_ref, *refs):
    out_refs, (totals, held, sems) = refs[:arrays], refs[arrays:]

    def prepare():
        totals[...] = jnp.zeros_like(totals)

    add_list(group, table_ref, x_ref, tiles_ref, held, totals, sems, prepare)
    write_totals(totals, out_refs)


def tile_scratch(tiles):
    _, edge, _ = tiles.shape
    return [pltpu.VMEM((SLOTS, UNROLL, edge, edge), BF16), pltpu.SemaphoreType.DMA((SLOTS,))]


def work(arrays):
    return pl.CostEstimate(
        flops=5_000_000_000 * arrays, bytes_accessed=5_000_000 * arrays, transcendentals=0
    )


def tile_products(group, arrays, table, x, tiles, rows):
    edge, width = tiles.shape[1], x.shape[1]
    return pl.pallas_call(
        functools.partial(tile_kernel, group, arrays),
        out_shape=[jax.ShapeDtypeStruct((rows, width), BF16)] * arrays,
        in_specs=[SMEM, VMEM, HBM],
        out_specs=[VMEM] * arrays,
        scratch_shapes=[pltpu.VMEM((arrays * rows + edge, width), F32), *tile_scratch(tiles)],
        compiler_params=params(32),
        cost_estimate=work(arrays),
        name="tile_products",
    )(table, x, tiles)


def early_products(group, arrays, table, pieces, x_rows, tiles, rows):
    edge, width = tiles.shape[1], pieces[0].shape[1]
    return pl.pallas_call(
        functools.partial(early_kernel, group, len(pieces)),
        out_shape=[
            jax.ShapeDtypeStruct((x_rows, width), BF16),
            jax.ShapeDtypeStruct((arrays * rows + edge, width), F32),
        ],
        in_specs=[SMEM] + [VMEM] * len(pieces) + [HBM],
        out_specs=[VMEM] * 2,
        scratch_shapes=tile_scratch(tiles),
        compiler_params=params(32),
        cost_estimate=work(1),
        name="early_products",
    )(table, *pieces, tiles)


def late_products(group, arrays, table, pieces, x, totals, tiles, rows):
    width = x.shape[1]
    at = len(pieces) + 2
    return pl.pallas_call(
        functools.partial(late_kernel, group, arrays, len(pieces)),
        out_shape=[
            jax.ShapeDtypeStruct(x.shape, x.dtype),
            jax.ShapeDtypeStruct(totals.shape, totals.dtype),
        ]
        + [jax.ShapeDtypeStruct((rows, width), BF16)] * arrays,
        in_specs=[SMEM] + [VMEM] * len(pieces) + [HBM, VMEM, VMEM],
        out_specs=[VMEM] * (2 + arrays),
        scratch_shapes=tile_scratch(tiles),
        input_output_aliases={at: 0, at + 1: 1},
        compiler_params=params(32),
        cost_estimate=work(1),
        name="late_products",
    )(table, *pieces, tiles, x, totals)


def wide(ref, start, rows):
    return ref[start : start + rows, :].astype(F32)


def forward_kernel(*refs):
    for stream in range(STREAMS):
        kept, got, out = refs[2 * stream], refs[2 * stream + 1], refs[2 * STREAMS + stream]
        out[...] = (kept[...].astype(F32) + got[...].astype(F32)).astype(BF16)


def forward_sums(kept, got):
    pairs = [array for pair in zip(kept, got) for array in pair]
    return pl.pallas_call(
        forward_kernel,
        out_shape=[jax.ShapeDtypeStruct(kept[0].shape, BF16)] * STREAMS,
        in_specs=[VMEM] * len(pairs),
        out_specs=[VMEM] * STREAMS,
        compiler_params=params(32),
        name="forward_sums",
    )(*pairs)


def turn_kernel(*refs):
    outs = refs[3 * PAIR :]
    for stream in range(PAIR):
        kept, got, last = refs[3 * stream : 3 * stream + 3]
        rows = last.shape[0] // SIDE
        at = stream * rows
        for delta in range(SIDE):
            start = delta * rows
            total = wide(kept, start, rows) + wide(got, start, rows) + wide(last, start, rows)
            out = outs[delta]
            out[at : at + rows, :] = total.astype(out.dtype)


def turn_sums(kept, got, last):
    ins = [array for three in zip(kept, got, last) for array in three]
    rows, width = last[0].shape
    shape = (PAIR * rows // SIDE, width)
    outs = [jax.ShapeDtypeStruct(shape, F32)] + [jax.ShapeDtypeStruct(shape, BF16)] * (SIDE - 1)
    return pl.pallas_call(
        turn_kernel,
        out_shape=outs,
        in_specs=[VMEM] * len(ins),
        out_specs=[VMEM] * SIDE,
        compiler_params=params(32),
        name="turn_sums",
    )(*ins)


def dense_kernel(*refs):
    weight_ref, bias_ref, out_ref = refs[2 * SIDE :]
    for side in range(2):
        own, *got = refs[side * SIDE : (side + 1) * SIDE]
        rows = own.shape[0]
        total = own[...]
        for ref in got:
            total += ref[...].astype(F32)
        hidden = jnp.dot(total.astype(BF16), weight_ref[...], preferred_element_type=F32)
        hidden = jnp.maximum(hidden + bias_ref[...], 0.0)
        out_ref[side * rows : (side + 1) * rows, :] = hidden.astype(BF16)


def dense(terms, weight, bias):
    return pl.pallas_call(
        dense_kernel,
        out_shape=jax.ShapeDtypeStruct((2 * terms[0].shape[0], weight.shape[1]), BF16),
        in_specs=[VMEM] * (len(terms) + 2),
        out_specs=VMEM,
        compiler_params=params(32),
        name="dense",
    )(*terms, weight, bias.reshape(1, -1))


def over(array, axis, bit):
    pairs = [(c, c ^ bit) for c in range(lax.axis_size(axis))]
    return lax.ppermute(array, axis, pairs)


def gather_first(low, high):
    one_low, three_low = over(low, "y", 1), over(low, "y", 3)
    one_high, three_high = over(high, "y", 1), over(high, "y", 3)
    other = [over(low, "core", 1), over(high, "core", 1)]
    far = [over(one_low, "y", 3), over(three_high, "y", 1)]
    halves = [one_low, one_high, three_low, three_high]
    near = [over(piece, "core", 1) for piece in halves]
    return [low, high, *other, *halves, *near], far


def swap(arrays, axis, first):
    return [
        lax.ppermute(array, axis, [(c, c ^ bit) for c in range(SIDE)])
        for array, bit in zip(arrays, (1, 3) if first else (3, 1))
    ]


def spread(sums, axis):
    mine, *send = sums
    got = [
        lax.ppermute(array, axis, [(c, c ^ bit) for c in range(SIDE)])
        for bit, array in enumerate(send, 1)
    ]
    return [mine, *got]


def body(features, new_index, tile_values, tile_index, tile_count, weight, bias):
    grid_rows = lax.axis_size("y") * lax.axis_size("core")
    grid_cols = lax.axis_size("x") * lax.axis_size("z")
    local_rows = features.shape[0]
    everyone = ("core", "y", "x", "z")
    capacity = 2 * local_rows // (grid_rows * grid_cols)
    tiles = tile_values[0, 0]
    row_tiles = local_rows * grid_cols // tiles.shape[1]
    assert row_tiles == 256 and grid_cols == SIDE * SIDE

    codes = tile_codes(
        tile_index[0, 0], *(lax.axis_index(axis) for axis in ("x", "z", "y", "core"))
    )
    packed = pack_rows(new_index, features, grid_rows, grid_cols, capacity)
    got = lax.all_to_all(packed, everyone, split_axis=0, concat_axis=0, tiled=True)
    table = plan_tiles(tile_count.reshape(1), codes)
    got, table = lax.optimization_barrier((got, table))
    half = local_rows // 2
    low, high = (place_rows(got, first, half) for first in (0, half))
    early, far = gather_first(low, high)

    rows = local_rows * grid_cols // 16
    axes = ("x", "z")
    pairs = (slice(0, PAIR), slice(PAIR, STREAMS))
    x_rows = local_rows * grid_rows
    x, totals = early_products(0, STREAMS, table, early, x_rows, tiles, rows)
    far, x, totals = lax.optimization_barrier((far, x, totals))
    late = [*far, *(over(piece, "core", 1) for piece in far)]
    x, _, *sent_on = late_products(3, STREAMS, table, late, x, totals, tiles, rows)
    got_on = [swap(sent_on[pair], axis, True) for pair, axis in zip(pairs, axes)]
    both = tile_products(1, 2 * STREAMS, table, x, tiles, rows)
    got_own = [swap(both[pair], axis, True) for pair, axis in zip(pairs, axes)]
    hand = forward_sums(both[STREAMS:], got_on[0] + got_on[1])
    got_last = [swap(hand[pair], axis, False) for pair, axis in zip(pairs, axes)]
    hand, table, got_own = lax.optimization_barrier((hand, table, got_own))
    kept = tile_products(2, STREAMS, table, x, tiles, rows)
    first = spread(turn_sums(kept[pairs[0]], got_own[0], got_last[0]), "z")
    second = spread(turn_sums(kept[pairs[1]], got_own[1], got_last[1]), "x")
    return dense(first + second, weight, bias)


def solution(mesh):
    fine = Mesh(mesh.devices.reshape(-1, 2, SIDE, SIDE), ("y", "core", "x", "z"))
    grid = (("y", "core"), ("x", "z"))
    flat = ("y", "core", "x", "z")
    in_specs = (
        P(flat, None),
        P(flat),
        P(*grid, None, None, None),
        P(*grid, None, None),
        P(*grid),
        P(),
        P(),
    )
    return jax.shard_map(
        body, mesh=fine, in_specs=in_specs, out_specs=P(flat, None), check_vma=False
    )
```

```python
import functools

import jax
import jax.numpy as jnp
from jax import lax
from jax.experimental import pallas as pl
from jax.experimental.pallas import tpu as pltpu
from jax.sharding import Mesh
from jax.sharding import PartitionSpec as P

EXTRA = 8
PICK = 1024
UNROLL = 20
SLOTS = 8
STREAMS = 4
PAIR = 2
SIDE = 4
LANES = 128
F32 = jnp.float32
BF16 = jnp.bfloat16


def iota(shape, axis):
    return lax.broadcasted_iota(jnp.int32, shape, axis)


def log2(size):
    assert size & (size - 1) == 0
    return size.bit_length() - 1


def params(mib, **rest):
    return pltpu.CompilerParams(vmem_limit_bytes=mib << 20, **rest)


VMEM = pl.BlockSpec(memory_space=pltpu.VMEM)
SMEM = pl.BlockSpec(memory_space=pltpu.SMEM)
HBM = pl.BlockSpec(memory_space=pltpu.HBM)


def pack_kernel(
    grid_rows,
    grid_cols,
    capacity,
    index_hbm,
    rows_hbm,
    out_ref,
    index_ref,
    rows_ref,
    hits_ref,
    marks_ref,
    sems,
):
    local_rows, width = rows_ref.shape
    index_copy = pltpu.make_async_copy(index_hbm, index_ref, sems.at[0])
    index_copy.start()
    copy = pltpu.make_async_copy(rows_hbm, rows_ref, sems.at[1])
    copy.start()
    peers = grid_rows * grid_cols
    lanes = (LANES, 2 * LANES)
    earlier = jnp.where(iota(lanes, 0) < iota(lanes, 1), 1.0, 0.0).astype(BF16)
    rank_lane = iota((LANES, LANES), 0) & (capacity - 1)
    seen = jnp.zeros((peers, LANES), F32)
    zero = jnp.zeros((LANES, LANES), F32)
    places = []
    index_copy.wait()
    for block in range(local_rows // LANES):
        here = slice(block * LANES, (block + 1) * LANES)
        index = index_ref[block : block + 1, :]
        owner = index >> log2(local_rows)
        slot = index & (local_rows - 1)
        row = owner & (grid_rows - 1)
        peer = ((row & 1) * (grid_rows // 2) + (row >> 1)) * grid_cols + (owner >> log2(grid_rows))
        hit = jnp.where(iota((peers, LANES), 0) == peer, 1.0, 0.0)
        hits_ref[:, here] = hit.astype(BF16)
        counts = jnp.dot(hit.astype(BF16), earlier, preferred_element_type=F32)
        rank = jnp.sum((counts[:, :LANES] + seen) * hit, axis=0, keepdims=True).astype(jnp.int32)
        seen = seen + counts[:, LANES:]
        places.append(peer * capacity + rank)
        same = rank_lane == rank
        high = jnp.where(same, ((slot >> 7) + 1).astype(F32), zero)
        low = jnp.where(same, (slot & 127).astype(F32), zero)
        marks_ref[:LANES, here] = high.astype(BF16)
        marks_ref[LANES:, here] = low.astype(BF16)
    marks = lax.dot_general(
        hits_ref[...], marks_ref[...], (((1,), (1,)), ((), ())), preferred_element_type=F32
    )
    at = iota((peers, EXTRA, LANES), 1)
    none = jnp.zeros((peers, EXTRA, LANES), F32)
    extra = jnp.where(
        at == 0,
        marks[:, :LANES].reshape(peers, 1, LANES) + none,
        jnp.where(at == 1, marks[:, LANES:].reshape(peers, 1, LANES) + none, none),
    )
    out_ref[:, capacity:, :] = extra.astype(BF16)
    place = jnp.concatenate(places, axis=1)
    part = PICK // capacity
    copy.wait()

    def pick_rows(step, carry):
        pick = (iota((PICK, local_rows), 0) + step * PICK == place).astype(F32).astype(BF16)
        rows = jnp.dot(pick, rows_ref[...], preferred_element_type=F32).astype(BF16)
        out_ref[pl.ds(step * part, part), 0:capacity, :] = rows.reshape(part, capacity, width)
        return carry

    lax.fori_loop(0, peers * capacity // PICK, pick_rows, 0)


def pack_rows(index, rows, grid_rows, grid_cols, capacity):
    peers = grid_rows * grid_cols
    local_rows, width = rows.shape
    return pl.pallas_call(
        functools.partial(pack_kernel, grid_rows, grid_cols, capacity),
        out_shape=jax.ShapeDtypeStruct((peers, capacity + EXTRA, width), BF16),
        in_specs=[HBM] * 2,
        out_specs=VMEM,
        scratch_shapes=[
            pltpu.VMEM((local_rows // LANES, LANES), jnp.int32),
            pltpu.VMEM((local_rows, width), BF16),
            pltpu.VMEM((peers, local_rows), BF16),
            pltpu.VMEM((2 * LANES, local_rows), BF16),
            pltpu.SemaphoreType.DMA((2,)),
        ],
        compiler_params=params(60),
        name="pack_rows",
    )(index.reshape(-1, LANES), rows)


def place_kernel(first, in_ref, out_ref, slot_ref, rows_ref):
    peers, held, width = in_ref.shape
    capacity = held - EXTRA
    per = LANES // capacity
    extra = in_ref[:, capacity:, :].astype(F32)
    high, low = extra[:, 0, :], extra[:, 1, :]
    slot_ref[...] = jnp.where(high > 0.5, (high - 1.0) * 128.0 + low, -1.0)
    rows_ref[...] = in_ref[:, 0:capacity, :].reshape(peers * capacity, width)
    which = iota((peers // per, LANES), 1) >> log2(capacity)
    slot = jnp.zeros((peers // per, LANES), F32)
    for i in range(per):
        slot = jnp.where(which == i, slot_ref[pl.ds(i, peers // per, stride=per), :], slot)
    slot = slot.astype(jnp.int32)
    slot = jnp.concatenate([slot[q : q + 1, :] for q in range(peers // per)], axis=1)

    def place_rows(step, carry):
        pick = (iota((PICK, peers * capacity), 0) + (first + step * PICK) == slot).astype(F32).astype(BF16)
        rows = jnp.dot(pick, rows_ref[...], preferred_element_type=F32)
        out_ref[pl.ds(pl.multiple_of(step * PICK, PICK), PICK), :] = rows.astype(BF16)
        return carry

    lax.fori_loop(0, out_ref.shape[0] // PICK, place_rows, 0)


def place_rows(got, first, rows):
    peers, held, width = got.shape
    return pl.pallas_call(
        functools.partial(place_kernel, first),
        out_shape=jax.ShapeDtypeStruct((rows, width), BF16),
        in_specs=[VMEM],
        out_specs=VMEM,
        scratch_shapes=[
            pltpu.VMEM((peers, LANES), F32),
            pltpu.VMEM((peers * (held - EXTRA), width), BF16),
        ],
        compiler_params=params(32),
        name="place_rows",
    )(got)


def tile_codes(index, me_x, me_z, me_y, me_core):
    row, col = index[0], index[1]
    owner = (((col >> 5) ^ me_y) << 1) | (((col >> 4) & 1) ^ me_core)
    block = (0x53764210 >> (4 * owner)) & 7
    col = (block << 4) | (col & 15)
    tile = jnp.arange(index.shape[1], dtype=jnp.int32)
    dest, inner = row >> 4, row & 15
    stream, sub = inner >> 2, inner & 3
    d_x, d_z = (dest >> 2) ^ me_x, (dest & 3) ^ me_z
    first = jnp.where(stream < 2, d_x, d_z)
    second = jnp.where(stream < 2, d_z, d_x)
    near = jnp.where(stream & 1 == 0, 1, 3)
    place = stream * 16 + second * 4 + sub
    group = jnp.where(first == 0, 2, jnp.where(first == 2, 0, 1))
    place = place + jnp.where((group == 1) & (first != near), 64, 0)
    group = jnp.where((group == 0) & (block >= 6), 3, group)
    return (group << 25) | (tile << 15) | (place << 7) | col


def plan_kernel(count_ref, code_ref, table_ref):
    for group in range(4):
        table_ref[4, group] = 0

    def visit(step, carry):
        for sub in range(8):
            code = code_ref[step * 8 + sub]
            group = code >> 25
            at = table_ref[4, group]
            table_ref[group, at] = code
            table_ref[4, group] = at + 1
        return carry

    count = count_ref[0]
    full = count // 8
    lax.fori_loop(0, full, visit, 0)

    def visit_one(tile, carry):
        code = code_ref[tile]
        group = code >> 25
        at = table_ref[4, group]
        table_ref[group, at] = code
        table_ref[4, group] = at + 1
        return carry

    lax.fori_loop(full * 8, count, visit_one, 0)
    for group in range(4):
        for step in range(UNROLL):
            table_ref[group, table_ref[4, group] + step] = 128 << 7


def plan_tiles(count, codes):
    return pl.pallas_call(
        plan_kernel,
        out_shape=jax.ShapeDtypeStruct((5, codes.shape[0] + UNROLL), jnp.int32),
        in_specs=[SMEM] * 2,
        out_specs=SMEM,
        name="plan_tiles",
    )(count, codes)


def add_list(group, table_ref, x_ref, tiles_ref, held, totals, sems, prepare):
    edge = held.shape[2]
    steps = (table_ref[4, group] + UNROLL - 1) // UNROLL

    def fetch(step):
        lane = lax.rem(step, SLOTS)
        for sub in range(UNROLL):
            tile = (table_ref[group, step * UNROLL + sub] >> 15) & 1023
            pltpu.make_async_copy(tiles_ref.at[tile], held.at[lane, sub], sems.at[lane]).start()

    for ahead in range(SLOTS - 1):

        @pl.when(ahead < steps)
        def _():
            fetch(ahead)

    prepare()

    def add_tiles(step, carry):
        @pl.when(step + SLOTS - 1 < steps)
        def _():
            fetch(step + SLOTS - 1)

        lane = lax.rem(step, SLOTS)
        pltpu.make_async_copy(tiles_ref.at[pl.ds(0, UNROLL)], held.at[lane], sems.at[lane]).wait()
        for sub in range(UNROLL):
            code = table_ref[group, step * UNROLL + sub]
            row = jnp.minimum((code >> 7) & 255, totals.shape[0] // edge - 1)
            col = code & 127
            product = jnp.dot(
                held[lane, sub],
                x_ref[pl.ds(pl.multiple_of(col * edge, edge), edge), :],
                preferred_element_type=F32,
            )
            totals[pl.ds(pl.multiple_of(row * edge, edge), edge), :] += product
        return carry

    lax.fori_loop(0, steps, add_tiles, 0)


def write_totals(totals, out_refs):
    rows = out_refs[0].shape[0]
    for array, out_ref in enumerate(out_refs):
        out_ref[...] = totals[array * rows : (array + 1) * rows, :].astype(BF16)


def join(pieces, out_ref, start):
    for piece in pieces:
        out_ref[start : start + piece.shape[0], :] = piece[...]
        start += piece.shape[0]


def early_kernel(group, pieces, table_ref, *refs):
    x_refs, (tiles_ref, x_out, totals, held, sems) = refs[:pieces], refs[pieces:]

    def prepare():
        totals[...] = jnp.zeros_like(totals)
        join(x_refs, x_out, 0)

    add_list(group, table_ref, x_out, tiles_ref, held, totals, sems, prepare)


def late_kernel(group, arrays, pieces, table_ref, *refs):
    x_refs, (tiles_ref, x_in, totals_in, x_out, totals), refs = (
        refs[:pieces],
        refs[pieces : pieces + 5],
        refs[pieces + 5 :],
    )
    out_refs, (held, sems) = refs[:arrays], refs[arrays:]
    rows = sum(piece.shape[0] for piece in x_refs)

    def prepare():
        join(x_refs, x_out, x_out.shape[0] - rows)

    add_list(group, table_ref, x_out, tiles_ref, held, totals, sems, prepare)
    write_totals(totals, out_refs)


def tile_kernel(group, arrays, table_ref, x_ref, tiles_ref, *refs):
    out_refs, (totals, held, sems) = refs[:arrays], refs[arrays:]

    def prepare():
        totals[...] = jnp.zeros_like(totals)

    add_list(group, table_ref, x_ref, tiles_ref, held, totals, sems, prepare)
    write_totals(totals, out_refs)


def tile_scratch(tiles):
    _, edge, _ = tiles.shape
    return [pltpu.VMEM((SLOTS, UNROLL, edge, edge), BF16), pltpu.SemaphoreType.DMA((SLOTS,))]


def work(arrays):
    return pl.CostEstimate(
        flops=5_000_000_000 * arrays, bytes_accessed=5_000_000 * arrays, transcendentals=0
    )


def tile_products(group, arrays, table, x, tiles, rows):
    edge, width = tiles.shape[1], x.shape[1]
    return pl.pallas_call(
        functools.partial(tile_kernel, group, arrays),
        out_shape=[jax.ShapeDtypeStruct((rows, width), BF16)] * arrays,
        in_specs=[SMEM, VMEM, HBM],
        out_specs=[VMEM] * arrays,
        scratch_shapes=[pltpu.VMEM((arrays * rows + edge, width), F32), *tile_scratch(tiles)],
        compiler_params=params(32),
        cost_estimate=work(arrays),
        name="tile_products",
    )(table, x, tiles)


def early_products(group, arrays, table, pieces, x_rows, tiles, rows):
    edge, width = tiles.shape[1], pieces[0].shape[1]
    return pl.pallas_call(
        functools.partial(early_kernel, group, len(pieces)),
        out_shape=[
            jax.ShapeDtypeStruct((x_rows, width), BF16),
            jax.ShapeDtypeStruct((arrays * rows + edge, width), F32),
        ],
        in_specs=[SMEM] + [VMEM] * len(pieces) + [HBM],
        out_specs=[VMEM] * 2,
        scratch_shapes=tile_scratch(tiles),
        compiler_params=params(32),
        cost_estimate=work(1),
        name="early_products",
    )(table, *pieces, tiles)


def late_products(group, arrays, table, pieces, x, totals, tiles, rows):
    width = x.shape[1]
    at = len(pieces) + 2
    return pl.pallas_call(
        functools.partial(late_kernel, group, arrays, len(pieces)),
        out_shape=[
            jax.ShapeDtypeStruct(x.shape, x.dtype),
            jax.ShapeDtypeStruct(totals.shape, totals.dtype),
        ]
        + [jax.ShapeDtypeStruct((rows, width), BF16)] * arrays,
        in_specs=[SMEM] + [VMEM] * len(pieces) + [HBM, VMEM, VMEM],
        out_specs=[VMEM] * (2 + arrays),
        scratch_shapes=tile_scratch(tiles),
        input_output_aliases={at: 0, at + 1: 1},
        compiler_params=params(32),
        cost_estimate=work(1),
        name="late_products",
    )(table, *pieces, tiles, x, totals)


def wide(ref, start, rows):
    return ref[start : start + rows, :].astype(F32)


def forward_kernel(*refs):
    for stream in range(STREAMS):
        kept, got, out = refs[2 * stream], refs[2 * stream + 1], refs[2 * STREAMS + stream]
        out[...] = (kept[...].astype(F32) + got[...].astype(F32)).astype(BF16)


def forward_sums(kept, got):
    pairs = [array for pair in zip(kept, got) for array in pair]
    return pl.pallas_call(
        forward_kernel,
        out_shape=[jax.ShapeDtypeStruct(kept[0].shape, BF16)] * STREAMS,
        in_specs=[VMEM] * len(pairs),
        out_specs=[VMEM] * STREAMS,
        compiler_params=params(32),
        name="forward_sums",
    )(*pairs)


def turn_kernel(*refs):
    outs = refs[3 * PAIR :]
    for stream in range(PAIR):
        kept, got, last = refs[3 * stream : 3 * stream + 3]
        rows = last.shape[0] // SIDE
        at = stream * rows
        for delta in range(SIDE):
            start = delta * rows
            total = wide(kept, start, rows) + wide(got, start, rows) + wide(last, start, rows)
            out = outs[delta]
            out[at : at + rows, :] = total.astype(out.dtype)


def turn_sums(kept, got, last):
    ins = [array for three in zip(kept, got, last) for array in three]
    rows, width = last[0].shape
    shape = (PAIR * rows // SIDE, width)
    outs = [jax.ShapeDtypeStruct(shape, F32)] + [jax.ShapeDtypeStruct(shape, BF16)] * (SIDE - 1)
    return pl.pallas_call(
        turn_kernel,
        out_shape=outs,
        in_specs=[VMEM] * len(ins),
        out_specs=[VMEM] * SIDE,
        compiler_params=params(32),
        name="turn_sums",
    )(*ins)


def dense_kernel(own, *refs):
    got, (weight_ref, bias_ref), out_ref = refs[: SIDE - 1], refs[SIDE - 1 : SIDE + 1], refs[-1]
    total = own[...]
    for ref in got:
        total += ref[...].astype(F32)
    hidden = jnp.dot(total.astype(BF16), weight_ref[...], preferred_element_type=F32)
    out_ref[...] = jnp.maximum(hidden + bias_ref[...], 0.0).astype(BF16)


def dense(side, terms, weight, bias, *done):
    rows, hidden = terms[0].shape[0], weight.shape[1]
    return pl.pallas_call(
        dense_kernel,
        grid=(1,),
        out_shape=jax.ShapeDtypeStruct((2 * rows, hidden), BF16),
        in_specs=[VMEM] * (SIDE + 2) + [pl.BlockSpec(memory_space=pl.ANY)] * len(done),
        out_specs=pl.BlockSpec((rows, hidden), lambda step: (side, 0)),
        input_output_aliases={SIDE + 2: 0} if done else {},
        compiler_params=params(32),
        name="dense",
    )(*terms, weight, bias.reshape(1, -1), *done)


def over(array, axis, bit):
    pairs = [(c, c ^ bit) for c in range(lax.axis_size(axis))]
    return lax.ppermute(array, axis, pairs)


def gather_first(low, high):
    one_low, three_low = over(low, "y", 1), over(low, "y", 3)
    one_high, three_high = over(high, "y", 1), over(high, "y", 3)
    other = [over(low, "core", 1), over(high, "core", 1)]
    far = [over(one_low, "y", 3), over(three_high, "y", 1)]
    halves = [one_low, one_high, three_low, three_high]
    near = [over(piece, "core", 1) for piece in halves]
    return [low, high, *other, *halves, *near], far


def swap(arrays, axis, first):
    return [
        lax.ppermute(array, axis, [(c, c ^ bit) for c in range(SIDE)])
        for array, bit in zip(arrays, (1, 3) if first else (3, 1))
    ]


def spread(sums, axis):
    mine, *send = sums
    got = [
        lax.ppermute(array, axis, [(c, c ^ bit) for c in range(SIDE)])
        for bit, array in enumerate(send, 1)
    ]
    return [mine, *got]


def body(features, new_index, tile_values, tile_index, tile_count, weight, bias):
    grid_rows = lax.axis_size("y") * lax.axis_size("core")
    grid_cols = lax.axis_size("x") * lax.axis_size("z")
    local_rows = features.shape[0]
    everyone = ("core", "y", "x", "z")
    capacity = 2 * local_rows // (grid_rows * grid_cols)
    tiles = tile_values[0, 0]
    row_tiles = local_rows * grid_cols // tiles.shape[1]
    assert row_tiles == 256 and grid_cols == SIDE * SIDE

    codes = tile_codes(
        tile_index[0, 0], *(lax.axis_index(axis) for axis in ("x", "z", "y", "core"))
    )
    packed = pack_rows(new_index, features, grid_rows, grid_cols, capacity)
    got = lax.all_to_all(packed, everyone, split_axis=0, concat_axis=0, tiled=True)
    table = plan_tiles(tile_count.reshape(1), codes)
    got, table = lax.optimization_barrier((got, table))
    half = local_rows // 2
    low, high = (place_rows(got, first, half) for first in (0, half))
    early, far = gather_first(low, high)

    rows = local_rows * grid_cols // 16
    axes = ("x", "z")
    pairs = (slice(0, PAIR), slice(PAIR, STREAMS))
    x_rows = local_rows * grid_rows
    x, totals = early_products(0, STREAMS, table, early, x_rows, tiles, rows)
    far, x, totals = lax.optimization_barrier((far, x, totals))
    late = [*far, *(over(piece, "core", 1) for piece in far)]
    x, _, *sent_on = late_products(3, STREAMS, table, late, x, totals, tiles, rows)
    got_on = [swap(sent_on[pair], axis, True) for pair, axis in zip(pairs, axes)]
    both = tile_products(1, 2 * STREAMS, table, x, tiles, rows)
    got_own = [swap(both[pair], axis, True) for pair, axis in zip(pairs, axes)]
    hand = forward_sums(both[STREAMS:], got_on[0] + got_on[1])
    got_last = [swap(hand[pair], axis, False) for pair, axis in zip(pairs, axes)]
    hand, table, got_own = lax.optimization_barrier((hand, table, got_own))
    kept = tile_products(2, STREAMS, table, x, tiles, rows)
    first = spread(turn_sums(kept[pairs[0]], got_own[0], got_last[0]), "z")
    second = spread(turn_sums(kept[pairs[1]], got_own[1], got_last[1]), "x")
    hidden = dense(0, first, weight, bias)
    return dense(1, second, weight, bias, hidden)


def solution(mesh):
    fine = Mesh(mesh.devices.reshape(-1, 2, SIDE, SIDE), ("y", "core", "x", "z"))
    grid = (("y", "core"), ("x", "z"))
    flat = ("y", "core", "x", "z")
    in_specs = (
        P(flat, None),
        P(flat),
        P(*grid, None, None, None),
        P(*grid, None, None),
        P(*grid),
        P(),
        P(),
    )
    return jax.shard_map(
        body, mesh=fine, in_specs=in_specs, out_specs=P(flat, None), check_vma=False
    )
```
